128 devices in a mesh: gx: 16 (over x_hi, y, core), gy: 8 (over z, x_lo).
Axes of the slice: x: 4 (x_hi: 2, x_lo: 2; x = x_hi * 2 + x_lo), y: 4, z: 4, core: 2. Of those that a mesh axis runs over, the one named last changes fastest.
Arguments:
- labels: int32 [128, 256, 64], P('gx', 'gy'), may hold values from 0 to 3
- seed_noise: float32 [4, 128, 256, 64], P(None, 'gx', 'gy'), may hold values from 0.05 to 1
- conc: float32 [128, 256, 64], P('gx', 'gy'), may hold values from 0.1 to 0.9
- curvature: float32 [4], replicated, may hold values from 1 to 4
- quartic: float32 [4], replicated, may hold values from 2 to 16
- wells: float32 [4], replicated, may hold values from 0.1 to 0.9
- lame: float32 [2, 4], replicated, may hold values from 0.5 to 2
- eigen: float32 [4, 6], replicated, may hold values from -3 to 3
Outputs:
- phase_next: float32 [4, 128, 256, 64], P(None, 'gx', 'gy')
- conc_next: float32 [128, 256, 64], P('gx', 'gy')
- stress: float32 [6, 128, 256, 64], P(None, 'gx', 'gy')
The draws below stay inside these ranges and needn't reach their ends.
All inputs are finite; a program needn't handle non-finite values.
Results may differ from the reference program's by a relative error of at most 0.0003.
Values sent between devices are 32-bit elements; how exact they have to be, the bound alone decides.
No kernel may reach another device: no remote copies, remote signals or barrier semaphores. Data moves between devices by JAX's collectives and lax.ppermute only.
A program may use at most 128 MiB of HBM per device.

```python
import math
import jax
import jax.numpy as jnp
from jax import lax

NZ = 64
NEWTON = 5
ITERS = 2
NX = 128
NY = 256


def touch_ends(values, key, smallest, top_value):
    index_at = [jax.random.randint(jax.random.fold_in(key, axis), (), 0, length) for axis, length in enumerate(values.shape)]
    main_axis = values.shape.index(max(values.shape))
    neighbour = index_at[:main_axis] + [(index_at[main_axis] + 1) % values.shape[main_axis]] + index_at[main_axis + 1:]
    return values.at[tuple(index_at)].set(smallest).at[tuple(neighbour)].set(top_value)


def levels(rng, shape, pieces, least, top_value):
    loudness, own = 1.0, jax.random.fold_in(rng, 6)
    for position, blocks in pieces:
        steps = jnp.exp(jax.random.uniform(jax.random.fold_in(own, position), (blocks,), jnp.float32, least / len(pieces), top_value / len(pieces)))
        loudness = loudness * jnp.repeat(steps, shape[position] // blocks).reshape([-1 if axis == position else 1 for axis in range(len(shape))])
    return loudness


def scatter_about(own_key, shape, width, reach, kind=jnp.bfloat16):
    return jnp.clip(width * jax.random.normal(own_key, shape, jnp.float32), -reach, reach).astype(kind)


def setup_inputs(seed: int = 0) -> dict:
    seeds = jax.random.split(jax.random.key(seed), 9)
    return {
        "labels": touch_ends(jax.random.randint(seeds[0], (NX, NY, NZ), 0, 4), jax.random.fold_in(seeds[0], 1), 0, 3).astype(jnp.int32),
        "seed_noise": jnp.clip(0.05 + 0.95 * jax.random.uniform(seeds[1], (4, NX, NY, NZ), jnp.float32) ** levels(seeds[1], (4, NX, NY, NZ), ((1, 16), (2, 8)), -0.2, 0.2), 0.05, 1.0),
        "conc": jnp.clip(0.1 + 0.79999997 * jax.random.uniform(seeds[2], (NX, NY, NZ), jnp.float32) ** levels(seeds[2], (NX, NY, NZ), ((0, 16), (1, 8)), -0.2, 0.2), 0.1, 0.9),
        "curvature": jnp.clip(jnp.exp(jax.random.uniform(seeds[3], (4,), jnp.float32, math.log(1.0), math.log(4.0))), 1.0, 4.0),
        "quartic": jnp.clip(jnp.exp(jax.random.uniform(seeds[4], (4,), jnp.float32, math.log(2.0), math.log(16.0))), 2.0, 16.0),
        "wells": jnp.clip(jax.random.uniform(seeds[5], (4,), jnp.float32, 0.1, 0.9), 0.1, 0.9),
        "lame": jnp.clip(jnp.exp(jax.random.uniform(seeds[6], (2, 4), jnp.float32, math.log(0.5), math.log(2.0))), 0.5, 2.0),
        "eigen": scatter_about(seeds[7], (4, 6), 0.3, 3.0, jnp.float32),
    }


step_phase = 0.06
step_conc = 0.005


def column(values):
    return values.reshape(4, 1, 1, 1)


def phases_from(labels, seed_noise):
    marks = lax.broadcasted_iota(jnp.int32, (4, 1, 1, 1), 0)
    raw = seed_noise + 2.0 * (labels[None] == marks).astype(seed_noise.dtype)
    return raw / jnp.sum(raw, axis=0, keepdims=True)


def partition(phase, conc, curvature, quartic, wells):
    coef_a = column(curvature)
    coef_b = column(quartic)
    centre = column(wells)
    part = jnp.broadcast_to(conc[None], phase.shape)
    deviate = part - centre
    chem = jnp.sum(phase * (coef_a * deviate + coef_b * deviate ** 3), axis=0)
    for _ in range(NEWTON):
        deviate = part - centre
        slope = coef_a * deviate + coef_b * deviate ** 3 - chem[None]
        stiff = coef_a + 3.0 * coef_b * deviate * deviate
        shift = (conc - jnp.sum(phase * part, axis=0) + jnp.sum(phase * slope / stiff, axis=0)) / jnp.sum(phase / stiff, axis=0)
        part = part + (shift[None] - slope) / stiff
        chem = chem + shift
    return part, chem


def stress_of(strain, eigen_field, lam_field, shear_field):
    elastic = strain - eigen_field
    trace = elastic[0] + elastic[1] + elastic[2]
    normal = (lax.broadcasted_iota(jnp.int32, (6, 1, 1, 1), 0) < 3).astype(strain.dtype)
    return 2.0 * shear_field[None] * elastic + (lam_field * trace)[None] * normal


def green(tau, freq_x, freq_y, freq_z, zero, lam0, mu0):
    vec_x = tau[0] * freq_x + tau[5] * freq_y + tau[4] * freq_z
    vec_y = tau[5] * freq_x + tau[1] * freq_y + tau[3] * freq_z
    vec_z = tau[4] * freq_x + tau[3] * freq_y + tau[2] * freq_z
    inner = freq_x * vec_x + freq_y * vec_y + freq_z * vec_z
    square = freq_x * freq_x + freq_y * freq_y + freq_z * freq_z + zero
    first = 1.0 / (2.0 * mu0 * square)
    second = (lam0 + mu0) / (mu0 * (lam0 + 2.0 * mu0)) * inner / (square * square)
    pairs = ((freq_x, vec_x, freq_x, vec_x), (freq_y, vec_y, freq_y, vec_y), (freq_z, vec_z, freq_z, vec_z),
             (freq_y, vec_y, freq_z, vec_z), (freq_x, vec_x, freq_z, vec_z), (freq_x, vec_x, freq_y, vec_y))
    result = [(fk * vh + fh * vk) * first - fk * fh * second for fk, vk, fh, vh in pairs]
    return jnp.stack(result, axis=0)


def signed_freq(length, axis, dtype):
    index = jnp.arange(length, dtype=jnp.int32)
    index = jnp.where(index >= length // 2, index - length, index)
    kept = jnp.where(index == -(length // 2), 0, index).astype(jnp.int32)
    dims_shape = [1, 1, 1]
    dims_shape[axis] = length
    return (kept.astype(dtype) / length).reshape(dims_shape)


def laplace(field):
    total = -6.0 * field
    for axis in (1, 2, 3):
        total = total + jnp.roll(field, 1, axis) + jnp.roll(field, -1, axis)
    return total


def reference(labels, seed_noise, conc, curvature, quartic, wells, lame, eigen):
    dtype = seed_noise.dtype
    phase = phases_from(labels, seed_noise)
    part, chem = partition(phase, conc, curvature, quartic, wells)
    lam_field = jnp.sum(phase * column(lame[0]), axis=0)
    shear_field = jnp.sum(phase * column(lame[1]), axis=0)
    eigen_field = jnp.einsum("ap,axyz->pxyz", eigen, phase, precision=lax.Precision.HIGHEST)
    lam0 = 0.5 * (jnp.max(lame[0]) + jnp.min(lame[0]))
    mu0 = 0.5 * (jnp.max(lame[1]) + jnp.min(lame[1]))
    freq_x = signed_freq(NX, 0, dtype)
    freq_y = signed_freq(NY, 1, dtype)
    freq_z = signed_freq(NZ, 2, dtype)
    zero = ((freq_x == 0.0) & (freq_y == 0.0) & (freq_z == 0.0)).astype(dtype)
    strain = jnp.zeros((6, NX, NY, NZ), dtype)
    for _ in range(ITERS):
        stress = stress_of(strain, eigen_field, lam_field, shear_field)
        spectrum = jnp.fft.fftn(stress, axes=(1, 2, 3))
        upd_real = green(jnp.real(spectrum), freq_x, freq_y, freq_z, zero, lam0, mu0)
        upd_imag = green(jnp.imag(spectrum), freq_x, freq_y, freq_z, zero, lam0, mu0)
        change = jnp.real(jnp.fft.ifftn(lax.complex(upd_real, upd_imag), axes=(1, 2, 3)))
        strain = strain - change.astype(dtype)
    stress = stress_of(strain, eigen_field, lam_field, shear_field)
    deviate = part - column(wells)
    energy = 0.5 * column(curvature) * deviate ** 2 + 0.25 * column(quartic) * deviate ** 4
    chemical = energy - chem[None] * part
    elastic = strain - eigen_field
    trace = elastic[0] + elastic[1] + elastic[2]
    squares = elastic[0] ** 2 + elastic[1] ** 2 + elastic[2] ** 2 + 2.0 * (elastic[3] ** 2 + elastic[4] ** 2 + elastic[5] ** 2)
    weight = jnp.array([1.0, 1.0, 1.0, 2.0, 2.0, 2.0], dtype)
    coupling = jnp.einsum("ap,pxyz->axyz", eigen * weight[None], stress, precision=lax.Precision.HIGHEST)
    stored = 0.5 * (column(lame[0]) * trace[None] ** 2 + 2.0 * column(lame[1]) * squares[None]) - coupling
    total_sq = jnp.sum(phase * phase, axis=0)
    barrier = 2.0 * phase * (total_sq[None] - phase * phase)
    force = chemical + stored + barrier - laplace(phase)
    phase_next = phase - step_phase * (force - jnp.mean(force, axis=0, keepdims=True))
    conc_next = conc + step_conc * laplace(chem[None])[0]
    return phase_next, conc_next, stress
```

```python
import numpy as np

import jax
import jax.numpy as jnp
from jax import lax
from jax.experimental import pallas as pl
from jax.experimental.pallas import tpu as pltpu
from jax.sharding import PartitionSpec as P

NEWTON = 5
STEP_PHASE = 0.06
STEP_CONC = 0.005

F32 = jnp.float32
BF16 = jnp.bfloat16

EVEN = (0, 1, 2, 5)
ODD = (3, 4)
ORDER = EVEN + ODD
BOTH = ("gx", "gy")


def split_np(table):
    high = table.astype(np.float32).astype(BF16)
    low = (table - high.astype(np.float64)).astype(np.float32).astype(BF16)
    return high, low


def z_tables():
    slab = np.arange(64)[:, None]
    z = np.arange(64)[None, :]
    freq = np.where(slab <= 32, slab, slab - 32)
    angle = 2.0 * np.pi * ((freq * z) % 64) / 64.0
    cos, sin = np.cos(angle), np.sin(angle)
    edge = (slab == 0) | (slab == 32)
    first = slab < 32
    even = np.where(edge | first, cos, sin)
    odd = np.where(edge | ~first, cos, sin)
    weight = np.where(edge, 1.0, 2.0) / 64.0

    def double(t):
        return np.kron(np.eye(2), t)

    return double(even), double(odd), double(even * weight), double(odd * weight)


def x_tables():
    order = np.array([8 * g + 4 * par + p for par in range(2) for p in range(4) for g in range(16)])
    k = np.arange(64)[:, None]
    angle = 2.0 * np.pi * ((k * order[None, :]) % 128) / 128.0
    real = np.cos(angle)
    imag = -np.sin(angle)
    imag[0] = np.where(order % 2 == 0, 1.0, -1.0)
    forward = np.concatenate([real, imag], axis=0)
    weight = np.where(np.arange(128) % 64 == 0, 1.0, 2.0) / (128.0 * 256.0)
    inverse = (forward * weight[:, None]).T
    return forward, inverse


def y_table():
    y = np.arange(256)
    angle = 2.0 * np.pi * ((y[:, None] * y[None, :]) % 256) / 256.0
    return np.concatenate([np.cos(angle), np.sin(angle)], axis=1)


def split(value):
    high = value.astype(BF16)
    low = (value - high.astype(F32)).astype(BF16)
    return high, low


def dot(a, b, dims=((1,), (0,))):
    return lax.dot_general(a, b, (dims, ((), ())), preferred_element_type=F32)


def dense(low, high):
    return jnp.concatenate([low, high], axis=-1)


def material(phase, lame, eigen):
    lam = sum(phase[a] * lame[0, a] for a in range(4))
    shear2 = sum(phase[a] * (2.0 * lame[1, a]) for a in range(4))
    eig = [sum(phase[a] * eigen[a, p] for a in range(4)) for p in range(6)]
    return lam, shear2, eig


def stress_from(elastic, lam, shear2):
    trace = lam * (elastic[0] + elastic[1] + elastic[2])
    return [shear2 * elastic[p] + trace if p < 3 else shear2 * elastic[p] for p in range(6)]


def put_split(values, row, size, high_ref, low_ref):
    for i, p in enumerate(ORDER):
        high, low = split(values[p])
        high_ref[pl.ds(i * 128 + row, size), :] = high
        low_ref[pl.ds(i * 128 + row, size), :] = low


NT = ((1,), (1,))


def z_forward(tab_ref, high_ref, low_ref, send_ref):
    for which, (start, comps) in enumerate(((0, EVEN), (512, ODD))):
        rows = 128 * len(comps)
        high = high_ref[pl.ds(start, rows), :]
        low = low_ref[pl.ds(start, rows), :]
        t_high, t_low = tab_ref[2 * which], tab_ref[2 * which + 1]
        out = dot(t_high, high, NT) + dot(t_high, low, NT) + dot(t_low, high, NT)
        for i, c in enumerate(comps):
            for par in range(2):
                piece = out[par * 64 : par * 64 + 64, i * 128 : i * 128 + 128]
                for r in range(2):
                    send_ref[pl.ds(r * 768 + c * 2 + par, 64, stride=12), :] = piece


def z_inverse(tab_ref, recv_ref, c):
    r, k = divmod(c, 3)
    pieces = [recv_ref[pl.ds(r * 384 + k * 2 + par, 64, stride=6), :] for par in range(2)]
    data = jnp.concatenate(pieces, axis=0).T
    which = 4 + 2 * (c in ODD)
    t_high, t_low = tab_ref[which], tab_ref[which + 1]
    high, low = split(data)
    return dot(high, t_high) + dot(low, t_high) + dot(high, t_low)


def first_kernel(labels_ref, noise_ref, lame, eigen, tab_ref, phase_ref, send_ref, high_ref, low_ref):
    for p in range(4):
        label = dense(labels_ref[p], labels_ref[p + 4])
        raw = [
            dense(noise_ref[a, p], noise_ref[a, p + 4]) + jnp.where(label == a, 2.0, 0.0).astype(F32)
            for a in range(4)
        ]
        inverse = 1.0 / (raw[0] + raw[1] + raw[2] + raw[3])
        phase = [raw[a] * inverse for a in range(4)]
        for a in range(4):
            phase_ref[a, pl.ds(p * 32, 32), :] = phase[a]
        lam, shear2, eig = material(phase, lame, eigen)
        stress = stress_from([-v for v in eig], lam, shear2)
        put_split(stress, p * 32, 32, high_ref, low_ref)
    z_forward(tab_ref, high_ref, low_ref, send_ref)


def middle_kernel(recv_ref, phase_ref, lame, eigen, tab_ref, strain_ref, send_ref, high_ref, low_ref):
    for c in range(6):
        strain_ref[c] = -z_inverse(tab_ref, recv_ref, c)
    for p in range(4):
        rows = pl.ds(p * 32, 32)
        phase = [phase_ref[a, rows, :] for a in range(4)]
        lam, shear2, eig = material(phase, lame, eigen)
        stress = stress_from([strain_ref[c, rows, :] - eig[c] for c in range(6)], lam, shear2)
        put_split(stress, p * 32, 32, high_ref, low_ref)
    z_forward(tab_ref, high_ref, low_ref, send_ref)


def last_kernel(recv_ref, phase_ref, strain_ref, force_ref, lame, eigen, tab_ref, next_ref, stress_ref, work_ref):
    for c in range(6):
        work_ref[c] = strain_ref[c] - z_inverse(tab_ref, recv_ref, c)
    for p in range(4):
        rows = pl.ds(p * 32, 32)
        phase = [phase_ref[a, rows, :] for a in range(4)]
        lam, shear2, eig = material(phase, lame, eigen)
        elastic = [work_ref[c, rows, :] - eig[c] for c in range(6)]
        stress = stress_from(elastic, lam, shear2)
        for c in range(6):
            stress_ref[c, p] = stress[c][:, :64]
            stress_ref[c, p + 4] = stress[c][:, 64:]
        trace = elastic[0] + elastic[1] + elastic[2]
        trace = 0.5 * trace * trace
        squares = (
            elastic[0] * elastic[0]
            + elastic[1] * elastic[1]
            + elastic[2] * elastic[2]
            + 2.0 * (elastic[3] * elastic[3] + elastic[4] * elastic[4] + elastic[5] * elastic[5])
        )
        force = []
        for a in range(4):
            coupling = sum(stress[c] * (eigen[a, c] * (1.0 if c < 3 else 2.0)) for c in range(6))
            force.append(force_ref[a, rows, :] + lame[0, a] * trace + lame[1, a] * squares - coupling)
        mean = 0.25 * (force[0] + force[1] + force[2] + force[3])
        for a in range(4):
            new = phase[a] - STEP_PHASE * (force[a] - mean)
            next_ref[a, p] = new[:, :64]
            next_ref[a, p + 4] = new[:, 64:]


def swap_blocks(x):
    lane = lax.broadcasted_iota(jnp.int32, x[0].shape, 1)
    wide = lane < 64
    narrow = (lane & 32) == 0
    a = [jnp.where(wide, x[i], pltpu.roll(x[i + 2], 64, 1)) for i in range(2)]
    b = [jnp.where(wide, pltpu.roll(x[i], 64, 1), x[i + 2]) for i in range(2)]
    out = []
    for first, second in (a, b):
        out.append(jnp.where(narrow, first, pltpu.roll(second, 32, 1)))
        out.append(jnp.where(narrow, pltpu.roll(first, 96, 1), second))
    return out


def slab_kernel(recv_ref, lame, xf_ref, xi_ref, y_ref, send_ref, in_ref, high_ref, low_ref, mid_ref):
    device = lax.axis_index("gx") * 8 + lax.axis_index("gy")
    slab = lax.rem(device, 64)
    upper = device >= 64
    omega = jnp.where(slab < 32, slab, 32 - slab).astype(F32) * (1.0 / 64.0)
    lam = [lame[0, a] for a in range(4)]
    mu = [lame[1, a] for a in range(4)]

    def middle(v):
        top = jnp.maximum(jnp.maximum(v[0], v[1]), jnp.maximum(v[2], v[3]))
        least = jnp.minimum(jnp.minimum(v[0], v[1]), jnp.minimum(v[2], v[3]))
        return 0.5 * (top + least)

    lam0, mu0 = middle(lam), middle(mu)

    for c in range(6):
        for par in range(2):
            for gh in range(2):
                pieces = [
                    recv_ref[pl.ds((4 * gh + i) * 12 + c * 2 + par, 16, stride=96), :] for i in range(4)
                ]
                for p, value in enumerate(swap_blocks(pieces)):
                    in_ref[c, pl.ds(par * 64 + p * 16, 16), pl.ds(gh * 128, 128)] = value
    xf_high, xf_low = xf_ref[0], xf_ref[1]
    for c in range(6):
        high, low = split(in_ref[c])
        out = dot(xf_high, high) + dot(xf_high, low) + dot(xf_low, high)
        high, low = split(out)
        high_ref[pl.ds(c * 128, 128), :] = high
        low_ref[pl.ds(c * 128, 128), :] = low
    y_high, y_low = y_ref[0], y_ref[1]
    mid_ref[...] = dot(high_ref[...], y_high) + dot(low_ref[...], y_high) + dot(high_ref[...], y_low)
    lane = lax.broadcasted_iota(jnp.int32, (8, 256), 1)
    index = jnp.where(lane >= 128, lane - 256, lane)
    wy = jnp.where(lane == 128, 0, index).astype(F32) * (1.0 / 256.0)
    row = lax.broadcasted_iota(jnp.int32, (8, 256), 0)
    half_mu = jnp.full((8, 256), 2.0 * mu0, F32)
    ratio = (lam0 + mu0) / jnp.full((8, 256), mu0 * (lam0 + 2.0 * mu0), F32)
    for tile in range(8):
        wx = (row + tile * 8).astype(F32) * (1.0 / 128.0)
        q = wx * wx + wy * wy + omega * omega
        q = jnp.where(q == 0.0, 1.0, q)
        first = 1.0 / (half_mu * q)
        second = ratio / (q * q)
        re, im = [], []
        for c in range(6):
            r_rows = pl.ds(c * 128 + tile * 8, 8)
            i_rows = pl.ds(c * 128 + 64 + tile * 8, 8)
            re.append(mid_ref[r_rows, :256] + mid_ref[i_rows, 256:])
            im.append(mid_ref[i_rows, :256] - mid_ref[r_rows, 256:])
        xx, yy, zz, yz, xz, xy = range(6)
        vx = (re[xx] * wx + re[xy] * wy + omega * im[xz], im[xx] * wx + im[xy] * wy - omega * re[xz])
        vy = (re[xy] * wx + re[yy] * wy + omega * im[yz], im[xy] * wx + im[yy] * wy - omega * re[yz])
        vz = (re[xz] * wx + re[yz] * wy - omega * im[zz], im[xz] * wx + im[yz] * wy + omega * re[zz])
        inner = (wx * vx[0] + wy * vy[0] + omega * vz[1], wx * vx[1] + wy * vy[1] - omega * vz[0])
        out = []
        for part in range(2):
            s = inner[part] * second
            fx, fy = vx[part] * first, vy[part] * first
            out_xx = wx * (2.0 * fx - wx * s)
            out_yy = wy * (2.0 * fy - wy * s)
            out_xy = wx * fy + wy * fx - wx * wy * s
            turned = vz[1] if part == 0 else -vz[0]
            out_zz = omega * (2.0 * turned * first - omega * s)
            sign = -1.0 if part == 0 else 1.0
            other = 1 - part
            s_other = inner[other] * second
            fz = vz[part] * first
            out_xz = wx * fz + sign * omega * (vx[other] * first - wx * s_other)
            out_yz = wy * fz + sign * omega * (vy[other] * first - wy * s_other)
            out.append((out_xx, out_yy, out_zz, out_yz, out_xz, out_xy))
        for k in range(3):
            for part in range(2):
                value = jnp.where(upper, out[part][3 + k], out[part][k])
                high, low = split(value)
                at = pl.ds(k * 128 + part * 64 + tile * 8, 8)
                high_ref[at, :] = high
                low_ref[at, :] = low
    high, low = high_ref[pl.ds(0, 384), :], low_ref[pl.ds(0, 384), :]
    mid_ref[pl.ds(0, 384), :] = dot(high, y_high) + dot(low, y_high) + dot(high, y_low)
    xi_high, xi_low = xi_ref[0], xi_ref[1]
    for k in range(3):
        r_rows, i_rows = pl.ds(k * 128, 64), pl.ds(k * 128 + 64, 64)
        real = mid_ref[r_rows, :256] - mid_ref[i_rows, 256:]
        imag = mid_ref[i_rows, :256] + mid_ref[r_rows, 256:]
        high, low = split(jnp.concatenate([real, imag], axis=0))
        out = dot(xi_high, high) + dot(xi_high, low) + dot(xi_low, high)
        for par in range(2):
            for gh in range(2):
                lanes = slice(gh * 128, gh * 128 + 128)
                pieces = [out[par * 64 + p * 16 : par * 64 + p * 16 + 16, lanes] for p in range(4)]
                for i, value in enumerate(swap_blocks(pieces)):
                    send_ref[pl.ds((4 * gh + i) * 6 + k * 2 + par, 16, stride=48), :] = value


def newton_kernel(conc_ref, phase_ref, curvature, quartic, wells, chem_ref, chemical_ref):
    for p in range(4):
        rows = pl.ds(p * 32, 32)
        conc = dense(conc_ref[p], conc_ref[p + 4])
        phase = [phase_ref[a, rows, :] for a in range(4)]
        part = [conc] * 4
        chem = jnp.zeros_like(conc)
        for a in range(4):
            dev = conc - wells[a]
            chem = chem + phase[a] * (dev * (curvature[a] + quartic[a] * dev * dev))
        for _ in range(NEWTON):
            top = conc
            bottom = jnp.zeros_like(conc)
            slope, recip = [], []
            for a in range(4):
                dev = part[a] - wells[a]
                square = quartic[a] * dev * dev
                g = dev * (curvature[a] + square) - chem
                d = 1.0 / (curvature[a] + 3.0 * square)
                slope.append(g)
                recip.append(d)
                top = top + phase[a] * (g * d - part[a])
                bottom = bottom + phase[a] * d
            shift = top / bottom
            part = [part[a] + (shift - slope[a]) * recip[a] for a in range(4)]
            chem = chem + shift
        chem_ref[0, p] = chem[:, :64]
        chem_ref[0, p + 4] = chem[:, 64:]
        total = sum(phase[a] * phase[a] for a in range(4))
        for a in range(4):
            dev = part[a] - wells[a]
            square = dev * dev
            energy = square * (0.5 * curvature[a] + 0.25 * quartic[a] * square)
            chemical_ref[a, rows, :] = energy - chem * part[a] + 2.0 * phase[a] * (total - phase[a] * phase[a])


def faces_kernel(phase_ref, chem_ref, xlow_ref, xhigh_ref, ylow_ref, yhigh_ref):
    for a in range(4):
        xlow_ref[a] = phase_ref[a, pl.ds(0, 32), :][:, :64]
        xhigh_ref[a] = phase_ref[a, pl.ds(96, 32), :][:, 64:]
        for p in range(4):
            first = phase_ref[a, pl.ds(p * 32, 8), :][0:1]
            last = phase_ref[a, pl.ds(p * 32 + 24, 8), :][7:8]
            ylow_ref[a, pl.ds(p, 1), :] = first[:, :64]
            ylow_ref[a, pl.ds(p + 4, 1), :] = first[:, 64:]
            yhigh_ref[a, pl.ds(p, 1), :] = last[:, :64]
            yhigh_ref[a, pl.ds(p + 4, 1), :] = last[:, 64:]
    xlow_ref[4] = chem_ref[0, 0]
    xhigh_ref[4] = chem_ref[0, 7]
    for x in range(8):
        ylow_ref[4, pl.ds(x, 1), :] = chem_ref[0, x, pl.ds(0, 1), :]
        yhigh_ref[4, pl.ds(x, 1), :] = chem_ref[0, x, pl.ds(31, 1), :]


def laplace_kernel(
    phase_ref, chem_ref, chemical_ref, conc_ref, xlow_ref, xhigh_ref, ylow_ref, yhigh_ref, force_ref, conc_out_ref
):
    lane = lax.broadcasted_iota(jnp.int32, (32, 128), 1)
    row = lax.broadcasted_iota(jnp.int32, (32, 128), 0)
    first_z = (lane & 63) == 0
    last_z = (lane & 63) == 63
    low_half = lane < 64
    for f in range(5):
        if f < 4:
            block = [phase_ref[f, pl.ds(p * 32, 32), :] for p in range(4)]
        else:
            block = [dense(chem_ref[0, p], chem_ref[0, p + 4]) for p in range(4)]
        before = xlow_ref[f]
        after = xhigh_ref[f]
        before = dense(before, before)
        after = dense(after, after)
        for p in range(4):
            here = block[p]
            total = -6.0 * here
            if p > 0:
                total = total + block[p - 1]
            else:
                total = total + jnp.where(low_half, before, pltpu.roll(block[3], 64, 1))
            if p < 3:
                total = total + block[p + 1]
            else:
                total = total + jnp.where(low_half, pltpu.roll(block[0], 64, 1), after)
            y_before = dense(ylow_ref[f, pl.ds(p, 1), :], ylow_ref[f, pl.ds(p + 4, 1), :])
            y_after = dense(yhigh_ref[f, pl.ds(p, 1), :], yhigh_ref[f, pl.ds(p + 4, 1), :])
            total = total + jnp.where(row == 0, y_before, pltpu.roll(here, 1, 0))
            total = total + jnp.where(row == 31, y_after, pltpu.roll(here, 31, 0))
            total = total + jnp.where(first_z, pltpu.roll(here, 65, 1), pltpu.roll(here, 1, 1))
            total = total + jnp.where(last_z, pltpu.roll(here, 63, 1), pltpu.roll(here, 127, 1))
            if f < 4:
                rows = pl.ds(p * 32, 32)
                force_ref[f, rows, :] = chemical_ref[f, rows, :] - total
            else:
                conc_out_ref[p] = conc_ref[p] + STEP_CONC * total[:, :64]
                conc_out_ref[p + 4] = conc_ref[p + 4] + STEP_CONC * total[:, 64:]


VMEM = pl.BlockSpec(memory_space=pltpu.VMEM)
SMEM = pl.BlockSpec(memory_space=pltpu.SMEM)
LIMIT = 12 * 1024 * 1024


def call(kernel, args, out, scratch=(), scalars=(), cost=4e6, name=None):
    specs = [SMEM if i in scalars else VMEM for i in range(len(args))]
    shapes = [jax.ShapeDtypeStruct(s, F32) for s in out]
    return pl.pallas_call(
        kernel,
        out_shape=shapes,
        in_specs=specs,
        out_specs=[VMEM] * len(out),
        scratch_shapes=list(scratch),
        compiler_params=pltpu.CompilerParams(vmem_limit_bytes=LIMIT),
        cost_estimate=pl.CostEstimate(flops=int(cost), bytes_accessed=int(cost), transcendentals=0),
        name=name,
    )(*args)


def exchange(x, rows):
    y = lax.all_to_all(x.reshape(128, 1, rows * 128), BOTH, 0, 0, tiled=True)
    return y.reshape(128 * rows, 128)


def shards(labels, seed_noise, conc, curvature, quartic, wells, lame, eigen):
    tables = [half for t in z_tables() for half in split_np(t)]
    z_tab = jnp.asarray(np.stack(tables))
    x_forward, x_inverse = x_tables()
    xf = jnp.asarray(np.stack(split_np(x_forward)))
    xi = jnp.asarray(np.stack(split_np(x_inverse)))
    yt = jnp.asarray(np.stack(split_np(y_table())))

    halves = [pltpu.VMEM((768, 128), BF16), pltpu.VMEM((768, 128), BF16)]
    plane_scratch = [
        pltpu.VMEM((6, 128, 256), F32),
        pltpu.VMEM((768, 256), BF16),
        pltpu.VMEM((768, 256), BF16),
        pltpu.VMEM((768, 512), F32),
    ]

    def plane(recv):
        (back,) = call(
            slab_kernel, (recv, lame, xf, xi, yt), [(768, 128)], plane_scratch, scalars=(1,), name="slab"
        )
        return back

    phase, send = call(
        first_kernel,
        (labels, seed_noise, lame, eigen, z_tab),
        [(4, 128, 128), (1536, 128)],
        halves,
        scalars=(2, 3),
        name="first",
    )
    recv = exchange(send, 12)

    chem, chemical = call(
        newton_kernel,
        (conc, phase, curvature, quartic, wells),
        [(1, 8, 32, 64), (4, 128, 128)],
        scalars=(2, 3, 4),
        cost=2e7,
        name="newton",
    )
    xlow, xhigh, ylow, yhigh = call(
        faces_kernel, (phase, chem), [(5, 32, 64), (5, 32, 64), (5, 8, 64), (5, 8, 64)], name="faces"
    )

    def shift(value, axis, step):
        count = lax.axis_size(axis)
        return lax.ppermute(value, axis, [(i, (i + step) % count) for i in range(count)])

    from_low = shift(xhigh, "gx", 1)
    from_high = shift(xlow, "gx", -1)
    y_from_low = shift(yhigh, "gy", 1)
    y_from_high = shift(ylow, "gy", -1)
    force, conc_next = call(
        laplace_kernel,
        (phase, chem, chemical, conc, from_low, from_high, y_from_low, y_from_high),
        [(4, 128, 128), (8, 32, 64)],
        name="laplace",
    )

    back = exchange(plane(recv), 6)
    strain, send = call(
        middle_kernel,
        (back, phase, lame, eigen, z_tab),
        [(6, 128, 128), (1536, 128)],
        halves,
        scalars=(2, 3),
        name="middle",
    )
    back = exchange(plane(exchange(send, 12)), 6)
    phase_next, stress = call(
        last_kernel,
        (back, phase, strain, force, lame, eigen, z_tab),
        [(4, 8, 32, 64), (6, 8, 32, 64)],
        [pltpu.VMEM((6, 128, 128), F32)],
        scalars=(4, 5),
        name="last",
    )
    return (phase_next, conc_next, stress)


def solution(mesh):
    in_specs = (
        P("gx", "gy", None),
        P(None, "gx", "gy", None),
        P("gx", "gy", None),
        P(),
        P(),
        P(),
        P(),
        P(),
    )
    out_specs = (P(None, "gx", "gy", None), P("gx", "gy", None), P(None, "gx", "gy", None))
    return jax.shard_map(shards, mesh=mesh, in_specs=in_specs, out_specs=out_specs, check_vma=False)
```

```python
import numpy as np

import jax
import jax.numpy as jnp
from jax import lax
from jax.experimental import pallas as pl
from jax.experimental.pallas import tpu as pltpu
from jax.sharding import PartitionSpec as P

NEWTON = 5
STEP_PHASE = 0.06
STEP_CONC = 0.005

F32 = jnp.float32
BF16 = jnp.bfloat16

EVEN = (0, 1, 2, 5)
ODD = (3, 4)
ORDER = EVEN + ODD
BOTH = ("gx", "gy")


def split_np(table):
    high = table.astype(np.float32).astype(BF16)
    low = (table - high.astype(np.float64)).astype(np.float32).astype(BF16)
    return high, low


def z_tables():
    slab = np.arange(64)[:, None]
    z = np.arange(64)[None, :]
    freq = np.where(slab <= 32, slab, slab - 32)
    angle = 2.0 * np.pi * ((freq * z) % 64) / 64.0
    cos, sin = np.cos(angle), np.sin(angle)
    edge = (slab == 0) | (slab == 32)
    first = slab < 32
    even = np.where(edge | first, cos, sin)
    odd = np.where(edge | ~first, cos, sin)
    weight = np.where(edge, 1.0, 2.0) / 64.0

    def double(t):
        return np.kron(np.eye(2), t)

    return double(even), double(odd), double(even * weight), double(odd * weight)


def x_tables():
    order = np.array([8 * g + 4 * par + p for par in range(2) for p in range(4) for g in range(16)])
    k = np.arange(64)[:, None]
    angle = 2.0 * np.pi * ((k * order[None, :]) % 128) / 128.0
    real = np.cos(angle)
    imag = -np.sin(angle)
    imag[0] = np.where(order % 2 == 0, 1.0, -1.0)
    forward = np.concatenate([real, imag], axis=0)
    weight = np.where(np.arange(128) % 64 == 0, 1.0, 2.0) / (128.0 * 256.0)
    inverse = (forward * weight[:, None]).T
    return forward, inverse


def y_table():
    y = np.arange(256)
    angle = 2.0 * np.pi * ((y[:, None] * y[None, :]) % 256) / 256.0
    return np.concatenate([np.cos(angle), np.sin(angle)], axis=1)


def split(value):
    high = value.astype(BF16)
    low = (value - high.astype(F32)).astype(BF16)
    return high, low


def dot(a, b, dims=((1,), (0,))):
    return lax.dot_general(a, b, (dims, ((), ())), preferred_element_type=F32)


def dense(low, high):
    return jnp.concatenate([low, high], axis=-1)


class Params:
    def __init__(self, ref):
        self.ref = ref

    def row(self, i):
        return self.ref[pl.ds(i, 1), :]

    def lame(self, i, a):
        return self.row(4 * i + a)

    def eigen(self, a, p):
        return self.row(8 + 6 * a + p)


def write_params(lame, eigen, ref):
    def middle(v):
        top = jnp.maximum(jnp.maximum(v[0], v[1]), jnp.maximum(v[2], v[3]))
        least = jnp.minimum(jnp.minimum(v[0], v[1]), jnp.minimum(v[2], v[3]))
        return 0.5 * (top + least)

    values = [lame[i, a] for i in range(2) for a in range(4)]
    values += [eigen[a, p] for a in range(4) for p in range(6)]
    values += [middle(values[0:4]), middle(values[4:8])]
    for i, value in enumerate(values):
        ref[pl.ds(i, 1), :] = jnp.full((1, 128), value, F32)


def material(phase, lame, eigen):
    lam = sum(phase[a] * lame(0, a) for a in range(4))
    shear2 = 2.0 * sum(phase[a] * lame(1, a) for a in range(4))
    eig = [sum(phase[a] * eigen(a, p) for a in range(4)) for p in range(6)]
    return lam, shear2, eig


def stress_from(elastic, lam, shear2):
    trace = lam * (elastic[0] + elastic[1] + elastic[2])
    return [shear2 * elastic[p] + trace if p < 3 else shear2 * elastic[p] for p in range(6)]


def put_split(values, row, size, high_ref, low_ref):
    for i, p in enumerate(ORDER):
        high, low = split(values[p])
        high_ref[pl.ds(i * 128 + row, size), :] = high
        low_ref[pl.ds(i * 128 + row, size), :] = low


NT = ((1,), (1,))


def z_forward(tab_ref, high_ref, low_ref, send_ref):
    for which, (start, comps) in enumerate(((0, EVEN), (512, ODD))):
        rows = 128 * len(comps)
        high = high_ref[pl.ds(start, rows), :]
        low = low_ref[pl.ds(start, rows), :]
        t_high, t_low = tab_ref[2 * which], tab_ref[2 * which + 1]
        out = dot(t_high, high, NT) + dot(t_high, low, NT) + dot(t_low, high, NT)
        for i, c in enumerate(comps):
            r, k = divmod(c, 3)
            for par in range(2):
                for sh in range(8):
                    at = par * 64 + sh * 8
                    piece = out[at : at + 8, i * 128 : i * 128 + 128]
                    send_ref[pl.ds((sh * 16 + r * 8) * 6 + k * 2 + par, 8, stride=6), :] = piece


def z_inverse(tab_ref, recv_ref, c):
    r, k = divmod(c, 3)
    pieces = [
        recv_ref[pl.ds((sh * 16 + r * 8) * 6 + k * 2 + par, 8, stride=6), :] for par in range(2) for sh in range(8)
    ]
    data = jnp.concatenate(pieces, axis=0).T
    which = 4 + 2 * (c in ODD)
    t_high, t_low = tab_ref[which], tab_ref[which + 1]
    high, low = split(data)
    return dot(high, t_high) + dot(low, t_high) + dot(high, t_low)


def first_kernel(
    labels_hbm,
    noise_hbm,
    lame_hbm,
    eigen_hbm,
    tab_hbm,
    phase_ref,
    send_ref,
    par_ref,
    labels_ref,
    noise_ref,
    lame_ref,
    eigen_ref,
    tab_ref,
    high_ref,
    low_ref,
    sem,
):
    copies = [
        pltpu.make_async_copy(source, target, sem.at[i])
        for i, (source, target) in enumerate(
            (
                (lame_hbm, lame_ref),
                (eigen_hbm, eigen_ref),
                (labels_hbm, labels_ref),
                (noise_hbm, noise_ref),
                (tab_hbm, tab_ref),
            )
        )
    ]
    for copy in copies:
        copy.start()
    for copy in copies[:4]:
        copy.wait()
    write_params(lame_ref, eigen_ref, par_ref)

    def lame(i, a):
        return lame_ref[i, a]

    def eigen(a, p):
        return eigen_ref[a, p]

    for p in range(4):
        label = dense(labels_ref[p], labels_ref[p + 4])
        raw = [
            dense(noise_ref[a, p], noise_ref[a, p + 4]) + jnp.where(label == a, 2.0, 0.0).astype(F32)
            for a in range(4)
        ]
        inverse = 1.0 / (raw[0] + raw[1] + raw[2] + raw[3])
        phase = [raw[a] * inverse for a in range(4)]
        for a in range(4):
            phase_ref[a, pl.ds(p * 32, 32), :] = phase[a]
        lam, shear2, eig = material(phase, lame, eigen)
        stress = stress_from([-v for v in eig], lam, shear2)
        put_split(stress, p * 32, 32, high_ref, low_ref)
    copies[4].wait()
    z_forward(tab_ref, high_ref, low_ref, send_ref)


def middle_kernel(recv_ref, phase_ref, par_ref, tab_ref, *refs):
    strain_ref, send_ref, high_ref, low_ref = refs[-4:]
    par = Params(par_ref)
    for c in range(6):
        strain_ref[c] = -z_inverse(tab_ref, recv_ref, c)
    for p in range(4):
        rows = pl.ds(p * 32, 32)
        phase = [phase_ref[a, rows, :] for a in range(4)]
        lam, shear2, eig = material(phase, par.lame, par.eigen)
        stress = stress_from([strain_ref[c, rows, :] - eig[c] for c in range(6)], lam, shear2)
        put_split(stress, p * 32, 32, high_ref, low_ref)
    z_forward(tab_ref, high_ref, low_ref, send_ref)


def last_kernel(
    recv_ref, phase_ref, strain_ref, force_ref, par_ref, tab_ref, next_hbm, stress_hbm, work_ref, next_ref, stress_ref, sem
):
    par = Params(par_ref)
    for c in range(6):
        work_ref[c] = strain_ref[c] - z_inverse(tab_ref, recv_ref, c)
    copies = []
    for p in range(4):
        rows = pl.ds(p * 32, 32)
        phase = [phase_ref[a, rows, :] for a in range(4)]
        lam, shear2, eig = material(phase, par.lame, par.eigen)
        elastic = [work_ref[c, rows, :] - eig[c] for c in range(6)]
        stress = stress_from(elastic, lam, shear2)
        for c in range(6):
            stress_ref[p, 0, c] = stress[c][:, :64]
            stress_ref[p, 1, c] = stress[c][:, 64:]
        trace = elastic[0] + elastic[1] + elastic[2]
        trace = 0.5 * trace * trace
        squares = (
            elastic[0] * elastic[0]
            + elastic[1] * elastic[1]
            + elastic[2] * elastic[2]
            + 2.0 * (elastic[3] * elastic[3] + elastic[4] * elastic[4] + elastic[5] * elastic[5])
        )
        doubled = [stress[c] if c < 3 else 2.0 * stress[c] for c in range(6)]
        force = []
        for a in range(4):
            coupling = sum(doubled[c] * par.eigen(a, c) for c in range(6))
            force.append(force_ref[a, rows, :] + par.lame(0, a) * trace + par.lame(1, a) * squares - coupling)
        mean = 0.25 * (force[0] + force[1] + force[2] + force[3])
        for a in range(4):
            new = phase[a] - STEP_PHASE * (force[a] - mean)
            next_ref[p, 0, a] = new[:, :64]
            next_ref[p, 1, a] = new[:, 64:]
        for half in range(2):
            x = p + 4 * half
            copies.append(pltpu.make_async_copy(stress_ref.at[p, half], stress_hbm.at[:, x], sem.at[2 * x]))
            copies.append(pltpu.make_async_copy(next_ref.at[p, half], next_hbm.at[:, x], sem.at[2 * x + 1]))
        for copy in copies[-4:]:
            copy.start()
    for copy in copies:
        copy.wait()


def swap_blocks(x):
    lane = lax.broadcasted_iota(jnp.int32, x[0].shape, 1)
    wide = lane < 64
    narrow = (lane & 32) == 0
    a = [jnp.where(wide, x[i], pltpu.roll(x[i + 2], 64, 1)) for i in range(2)]
    b = [jnp.where(wide, pltpu.roll(x[i], 64, 1), x[i + 2]) for i in range(2)]
    out = []
    for first, second in (a, b):
        out.append(jnp.where(narrow, first, pltpu.roll(second, 32, 1)))
        out.append(jnp.where(narrow, pltpu.roll(first, 96, 1), second))
    return out


def spectrum_kernel(recv_ref, xf_ref, y_ref, *refs):
    out_ref, high_ref, low_ref, mid_ref = refs[-4:]
    xf_high, xf_low = xf_ref[0], xf_ref[1]
    for k in range(3):
        rows = []
        for par in range(2):
            columns = []
            for gh in range(2):
                pieces = [
                    recv_ref[pl.ds((4 * gh + i) * 6 + k * 2 + par, 16, stride=48), :] for i in range(4)
                ]
                columns.append(swap_blocks(pieces))
            rows += [jnp.concatenate([columns[0][p], columns[1][p]], axis=1) for p in range(4)]
        high, low = split(jnp.concatenate(rows, axis=0))
        out = dot(xf_high, high) + dot(xf_high, low) + dot(xf_low, high)
        high, low = split(out)
        high_ref[pl.ds(k * 128, 128), :] = high
        low_ref[pl.ds(k * 128, 128), :] = low
    y_high, y_low = y_ref[0], y_ref[1]
    mid_ref[...] = dot(high_ref[...], y_high) + dot(low_ref[...], y_high) + dot(high_ref[...], y_low)
    for k in range(3):
        real, imag = pl.ds(k * 128, 64), pl.ds(k * 128 + 64, 64)
        out_ref[real, :] = mid_ref[real, :256] + mid_ref[imag, 256:]
        out_ref[imag, :] = mid_ref[imag, :256] - mid_ref[real, 256:]


def green_tile(re, im, wx, wy, omega, first, second, upper):
    xx, yy, zz, yz, xz, xy = range(6)
    vx = (re[xx] * wx + re[xy] * wy + omega * im[xz], im[xx] * wx + im[xy] * wy - omega * re[xz])
    vy = (re[xy] * wx + re[yy] * wy + omega * im[yz], im[xy] * wx + im[yy] * wy - omega * re[yz])
    vz = (re[xz] * wx + re[yz] * wy - omega * im[zz], im[xz] * wx + im[yz] * wy + omega * re[zz])
    inner = (wx * vx[0] + wy * vy[0] + omega * vz[1], wx * vx[1] + wy * vy[1] - omega * vz[0])
    s = [inner[part] * second for part in range(2)]
    fx = [vx[part] * first for part in range(2)]
    fy = [vy[part] * first for part in range(2)]
    fz = [vz[part] * first for part in range(2)]
    out = []
    for part in range(2):
        other = 1 - part
        if upper:
            sign = -omega if part == 0 else omega
            out.append(
                (
                    wy * fz[part] + sign * (fy[other] - wy * s[other]),
                    wx * fz[part] + sign * (fx[other] - wx * s[other]),
                    wx * (fy[part] - wy * s[part]) + wy * fx[part],
                )
            )
        else:
            turned = fz[1] if part == 0 else -fz[0]
            out.append(
                (
                    wx * (2.0 * fx[part] - wx * s[part]),
                    wy * (2.0 * fy[part] - wy * s[part]),
                    omega * (2.0 * turned - omega * s[part]),
                )
            )
    return out


def green_kernel(own_ref, other_ref, after_ref, par_ref, xi_ref, y_ref, send_ref, high_ref, low_ref, mid_ref):
    del after_ref
    x_index, y_index = lax.axis_index("gx"), lax.axis_index("gy")
    core = lax.rem(x_index, 2)
    slab = lax.div(x_index, 2) * 8 + y_index
    omega = jnp.where(slab < 32, slab, 32 - slab).astype(F32) * (1.0 / 64.0)
    par = Params(par_ref)
    lam0 = jnp.concatenate([par.row(32), par.row(32)], axis=1)
    mu0 = jnp.concatenate([par.row(33), par.row(33)], axis=1)
    half_mu = 0.5 / mu0
    ratio = (lam0 + mu0) / (mu0 * (lam0 + 2.0 * mu0))
    lane = lax.broadcasted_iota(jnp.int32, (8, 256), 1)
    index = jnp.where(lane >= 128, lane - 256, lane)
    wy = jnp.where(lane == 128, 0, index).astype(F32) * (1.0 / 256.0)
    row = lax.broadcasted_iota(jnp.int32, (8, 256), 0)

    def green(upper):
        for tile in range(8):
            wx = (row + tile * 8).astype(F32) * (1.0 / 128.0)
            q = wx * wx + wy * wy + omega * omega
            inverse = 1.0 / jnp.where(q == 0.0, 1.0, q)
            first = half_mu * inverse
            second = ratio * inverse * inverse

            def get(ref, part):
                return [ref[pl.ds(k * 128 + part * 64 + tile * 8, 8), :] for k in range(3)]

            low, high = (other_ref, own_ref) if upper else (own_ref, other_ref)
            re, im = (get(low, part) + get(high, part) for part in range(2))
            out = green_tile(re, im, wx, wy, omega, first, second, upper)
            for part in range(2):
                for k in range(3):
                    high, low = split(out[part][k])
                    at = pl.ds(k * 128 + part * 64 + tile * 8, 8)
                    high_ref[at, :] = high
                    low_ref[at, :] = low

    @pl.when(core == 0)
    def _():
        green(False)

    @pl.when(core == 1)
    def _():
        green(True)

    y_high, y_low = y_ref[0], y_ref[1]
    mid_ref[...] = dot(high_ref[...], y_high) + dot(low_ref[...], y_high) + dot(high_ref[...], y_low)
    xi_high, xi_low = xi_ref[0], xi_ref[1]
    for k in range(3):
        r_rows, i_rows = pl.ds(k * 128, 64), pl.ds(k * 128 + 64, 64)
        real = mid_ref[r_rows, :256] - mid_ref[i_rows, 256:]
        imag = mid_ref[i_rows, :256] + mid_ref[r_rows, 256:]
        high, low = split(jnp.concatenate([real, imag], axis=0))
        out = dot(xi_high, high) + dot(xi_high, low) + dot(xi_low, high)
        for parity in range(2):
            for gh in range(2):
                lanes = slice(gh * 128, gh * 128 + 128)
                pieces = [out[parity * 64 + p * 16 : parity * 64 + p * 16 + 16, lanes] for p in range(4)]
                for i, value in enumerate(swap_blocks(pieces)):
                    send_ref[pl.ds((4 * gh + i) * 6 + k * 2 + parity, 16, stride=48), :] = value


def newton_kernel(
    conc_ref, phase_ref, curvature, quartic, wells, chem_ref, chemical_ref, xlow_ref, xhigh_ref, ylow_ref, yhigh_ref
):
    for p in range(4):
        rows = pl.ds(p * 32, 32)
        conc = dense(conc_ref[p], conc_ref[p + 4])
        phase = [phase_ref[a, rows, :] for a in range(4)]
        part = [conc] * 4
        chem = jnp.zeros_like(conc)
        for a in range(4):
            dev = conc - wells[a]
            chem = chem + phase[a] * (dev * (curvature[a] + quartic[a] * dev * dev))
        for _ in range(NEWTON):
            top = conc
            bottom = jnp.zeros_like(conc)
            slope, recip = [], []
            for a in range(4):
                dev = part[a] - wells[a]
                square = quartic[a] * dev * dev
                g = dev * (curvature[a] + square) - chem
                d = 1.0 / (curvature[a] + 3.0 * square)
                slope.append(g)
                recip.append(d)
                top = top + phase[a] * (g * d - part[a])
                bottom = bottom + phase[a] * d
            shift = top / bottom
            part = [part[a] + (shift - slope[a]) * recip[a] for a in range(4)]
            chem = chem + shift
        chem_ref[rows, :] = chem
        total = sum(phase[a] * phase[a] for a in range(4))
        for a in range(4):
            dev = part[a] - wells[a]
            square = dev * dev
            energy = square * (0.5 * curvature[a] + 0.25 * quartic[a] * square)
            chemical_ref[a, rows, :] = energy - chem * part[a] + 2.0 * phase[a] * (total - phase[a] * phase[a])
    low_half = lax.broadcasted_iota(jnp.int32, (32, 128), 1) < 64

    def field(f, rows):
        return phase_ref[f, rows, :] if f < 4 else chem_ref[rows, :]

    first, last = pl.ds(0, 32), pl.ds(96, 32)
    for j in range(2):
        at = pl.ds(j * 32, 32)
        xlow_ref[at, :] = jnp.where(low_half, field(2 * j, first), pltpu.roll(field(2 * j + 1, first), 64, 1))
        xhigh_ref[at, :] = jnp.where(low_half, pltpu.roll(field(2 * j, last), 64, 1), field(2 * j + 1, last))
    xlow_ref[pl.ds(64, 32), :] = field(4, first)
    xhigh_ref[pl.ds(64, 32), :] = pltpu.roll(field(4, last), 64, 1)
    for f in range(5):
        for p in range(4):
            ylow_ref[pl.ds(f * 4 + p, 1), :] = field(f, pl.ds(p * 32, 1))
            yhigh_ref[pl.ds(f * 4 + p, 1), :] = field(f, pl.ds(p * 32 + 31, 1))
    pad = jnp.zeros((4, 128), F32)
    ylow_ref[pl.ds(20, 4), :] = pad
    yhigh_ref[pl.ds(20, 4), :] = pad


def laplace_kernel(
    phase_ref,
    chem_ref,
    chemical_ref,
    conc_ref,
    xlow_ref,
    xhigh_ref,
    ylow_ref,
    yhigh_ref,
    after_ref,
    force_ref,
    conc_out_ref,
):
    del after_ref
    lane = lax.broadcasted_iota(jnp.int32, (32, 128), 1)
    row = lax.broadcasted_iota(jnp.int32, (32, 128), 0)
    first_z = (lane & 63) == 0
    last_z = (lane & 63) == 63
    low_half = lane < 64
    for f in range(5):
        block = [phase_ref[f, pl.ds(p * 32, 32), :] if f < 4 else chem_ref[pl.ds(p * 32, 32), :] for p in range(4)]
        at = pl.ds(f // 2 * 32, 32)
        before, after = xlow_ref[at, :], xhigh_ref[at, :]
        if f % 2 == 0:
            after = pltpu.roll(after, 64, 1)
        else:
            before = pltpu.roll(before, 64, 1)
        for p in range(4):
            here = block[p]
            total = -6.0 * here
            if p > 0:
                total = total + block[p - 1]
            else:
                total = total + jnp.where(low_half, before, pltpu.roll(block[3], 64, 1))
            if p < 3:
                total = total + block[p + 1]
            else:
                total = total + jnp.where(low_half, pltpu.roll(block[0], 64, 1), after)
            y_before = ylow_ref[pl.ds(f * 4 + p, 1), :]
            y_after = yhigh_ref[pl.ds(f * 4 + p, 1), :]
            total = total + jnp.where(row == 0, y_before, pltpu.roll(here, 1, 0))
            total = total + jnp.where(row == 31, y_after, pltpu.roll(here, 31, 0))
            total = total + jnp.where(first_z, pltpu.roll(here, 65, 1), pltpu.roll(here, 1, 1))
            total = total + jnp.where(last_z, pltpu.roll(here, 63, 1), pltpu.roll(here, 127, 1))
            if f < 4:
                rows = pl.ds(p * 32, 32)
                force_ref[f, rows, :] = chemical_ref[f, rows, :] - total
            else:
                conc_out_ref[p] = conc_ref[p] + STEP_CONC * total[:, :64]
                conc_out_ref[p + 4] = conc_ref[p + 4] + STEP_CONC * total[:, 64:]


VMEM = pl.BlockSpec(memory_space=pltpu.VMEM)
SMEM = pl.BlockSpec(memory_space=pltpu.SMEM)
HBM = pl.BlockSpec(memory_space=pltpu.HBM)
ANY = pl.BlockSpec(memory_space=pl.ANY)
LIMIT = 12 * 1024 * 1024


def call(kernel, args, out, scratch=(), special=None, out_spec=VMEM, cost=4e6, name=None):
    special = special or {}
    specs = [special.get(i, VMEM) for i in range(len(args))]
    shapes = [jax.ShapeDtypeStruct(s, F32) for s in out]
    return pl.pallas_call(
        kernel,
        out_shape=shapes,
        in_specs=specs,
        out_specs=[out_spec] * len(out),
        scratch_shapes=list(scratch),
        compiler_params=pltpu.CompilerParams(vmem_limit_bytes=LIMIT),
        cost_estimate=pl.CostEstimate(flops=int(cost), bytes_accessed=int(cost), transcendentals=0),
        name=name,
    )(*args)


def exchange(x):
    y = lax.all_to_all(x.reshape(128, 1, 768), BOTH, 0, 0, tiled=True)
    return y.reshape(768, 128)


def shards(labels, seed_noise, conc, curvature, quartic, wells, lame, eigen):
    tables = [half for t in z_tables() for half in split_np(t)]
    z_tab = jnp.asarray(np.stack(tables))
    x_forward, x_inverse = x_tables()
    xf = jnp.asarray(np.stack(split_np(x_forward)))
    xi = jnp.asarray(np.stack(split_np(x_inverse)))
    yt = jnp.asarray(np.stack(split_np(y_table())))

    halves = [pltpu.VMEM((768, 128), BF16), pltpu.VMEM((768, 128), BF16)]
    plane_scratch = [
        pltpu.VMEM((384, 256), BF16),
        pltpu.VMEM((384, 256), BF16),
        pltpu.VMEM((384, 512), F32),
    ]

    def shift(value, axis, step):
        count = lax.axis_size(axis)
        return lax.ppermute(value, axis, [(i, (i + step) % count) for i in range(count)])

    def spectrum(recv, after):
        (own,) = call(
            spectrum_kernel,
            (recv, xf, yt, *after),
            [(384, 256)],
            plane_scratch,
            {3 + i: ANY for i in range(len(after))},
            name="spectrum",
        )
        return own, lax.ppermute(own, "gx", [(i, i ^ 1) for i in range(16)])

    def update(own, other, after, par):
        (back,) = call(
            green_kernel,
            (own, other, after, par, xi, yt),
            [(768, 128)],
            plane_scratch,
            {2: ANY},
            name="green",
        )
        return exchange(back)

    def in_hbm(*arrays):
        return tuple(pltpu.with_memory_space_constraint(a, pltpu.HBM) for a in arrays)

    phase, send, par = call(
        first_kernel,
        in_hbm(labels, seed_noise, lame, eigen, z_tab),
        [(4, 128, 128), (768, 128), (40, 128)],
        [
            pltpu.VMEM((8, 32, 64), jnp.int32),
            pltpu.VMEM((4, 8, 32, 64), F32),
            pltpu.SMEM((2, 4), F32),
            pltpu.SMEM((4, 6), F32),
            pltpu.VMEM((8, 128, 128), BF16),
            *halves,
            pltpu.SemaphoreType.DMA((5,)),
        ],
        {i: HBM for i in range(5)},
        name="first",
    )
    recv = exchange(send)

    chem, chemical, xlow, xhigh, ylow, yhigh = call(
        newton_kernel,
        (conc, phase, curvature, quartic, wells),
        [(128, 128), (4, 128, 128), (96, 128), (96, 128), (24, 128), (24, 128)],
        special={2: SMEM, 3: SMEM, 4: SMEM},
        name="newton",
    )
    halo = [shift(xhigh, "gx", 1), shift(yhigh, "gy", 1), shift(xlow, "gx", -1), shift(ylow, "gy", -1)]
    halo = [halo[0], halo[2], halo[1], halo[3]]

    own, other = spectrum(recv, (ylow,))
    back = update(own, other, par, par)
    strain, send = call(
        middle_kernel,
        (back, phase, par, z_tab, *halo),
        [(6, 128, 128), (768, 128)],
        halves,
        {4 + i: ANY for i in range(4)},
        name="middle",
    )
    own, other = spectrum(exchange(send), ())
    force, conc_next = call(
        laplace_kernel,
        (phase, chem, chemical, conc, *halo, own),
        [(4, 128, 128), (8, 32, 64)],
        special={8: ANY},
        name="laplace",
    )
    back = update(own, other, force, par)
    phase_next, stress = call(
        last_kernel,
        (back, phase, strain, force, par, z_tab),
        [(4, 8, 32, 64), (6, 8, 32, 64)],
        [
            pltpu.VMEM((6, 128, 128), F32),
            pltpu.VMEM((4, 2, 4, 32, 64), F32),
            pltpu.VMEM((4, 2, 6, 32, 64), F32),
            pltpu.SemaphoreType.DMA((16,)),
        ],
        out_spec=HBM,
        name="last",
    )
    return (phase_next, conc_next, stress)


def solution(mesh):
    in_specs = (
        P("gx", "gy", None),
        P(None, "gx", "gy", None),
        P("gx", "gy", None),
        P(),
        P(),
        P(),
        P(),
        P(),
    )
    out_specs = (P(None, "gx", "gy", None), P("gx", "gy", None), P(None, "gx", "gy", None))
    return jax.shard_map(shards, mesh=mesh, in_specs=in_specs, out_specs=out_specs, check_vma=False)
```

```python
import numpy as np

import jax
import jax.numpy as jnp
from jax import lax
from jax.experimental import pallas as pl
from jax.experimental.pallas import tpu as pltpu
from jax.sharding import PartitionSpec as P


NEWTON = 5
STEP_PHASE = 0.06
STEP_CONC = 0.005

F32 = jnp.float32
BF16 = jnp.bfloat16

EVEN = (0, 1, 2, 5)
ODD = (3, 4)
ORDER = EVEN + ODD
BOTH = ("gx", "gy")


def split_np(table):
    high = table.astype(np.float32).astype(BF16)
    low = (table - high.astype(np.float64)).astype(np.float32).astype(BF16)
    return high, low


def z_tables():
    slab = np.arange(64)[:, None]
    z = np.arange(64)[None, :]
    freq = np.where(slab <= 32, slab, slab - 32)
    angle = 2.0 * np.pi * ((freq * z) % 64) / 64.0
    cos, sin = np.cos(angle), np.sin(angle)
    edge = (slab == 0) | (slab == 32)
    first = slab < 32
    even = np.where(edge | first, cos, sin)
    odd = np.where(edge | ~first, cos, sin)
    weight = np.where(edge, 1.0, 2.0) / 64.0

    def double(t):
        return np.kron(np.eye(2), t)

    return double(even), double(odd), double(even * weight), double(odd * weight)


def x_tables():
    order = np.array([8 * g + 4 * par + p for par in range(2) for p in range(4) for g in range(16)])
    k = np.arange(64)[:, None]
    angle = 2.0 * np.pi * ((k * order[None, :]) % 128) / 128.0
    real = np.cos(angle)
    imag = -np.sin(angle)
    imag[0] = np.where(order % 2 == 0, 1.0, -1.0)
    forward = np.concatenate([real, imag], axis=0)
    weight = np.where(np.arange(128) % 64 == 0, 1.0, 2.0) / (128.0 * 256.0)
    inverse = (forward * weight[:, None]).T
    return forward, inverse


def y_table():
    y = np.arange(256)
    angle = 2.0 * np.pi * ((y[:, None] * y[None, :]) % 256) / 256.0
    return np.concatenate([np.cos(angle), np.sin(angle)], axis=1)


def split(value):
    high = value.astype(BF16)
    low = (value - high.astype(F32)).astype(BF16)
    return high, low


def dot(a, b, dims=((1,), (0,))):
    return lax.dot_general(a, b, (dims, ((), ())), preferred_element_type=F32)


def dense(low, high):
    return jnp.concatenate([low, high], axis=-1)


class Params:
    def __init__(self, ref):
        self.ref = ref

    def row(self, i):
        return self.ref[pl.ds(i, 1), :]

    def lame(self, i, a):
        return self.row(4 * i + a)

    def eigen(self, a, p):
        return self.row(8 + 6 * a + p)


def write_params(lame, eigen, ref):
    def middle(v):
        top = jnp.maximum(jnp.maximum(v[0], v[1]), jnp.maximum(v[2], v[3]))
        least = jnp.minimum(jnp.minimum(v[0], v[1]), jnp.minimum(v[2], v[3]))
        return 0.5 * (top + least)

    values = [lame[i, a] for i in range(2) for a in range(4)]
    values += [eigen[a, p] for a in range(4) for p in range(6)]
    values += [middle(values[0:4]), middle(values[4:8])]
    for i, value in enumerate(values):
        ref[pl.ds(i, 1), :] = jnp.full((1, 128), value, F32)


def material(phase, lame, eigen):
    lam = sum(phase[a] * lame(0, a) for a in range(4))
    shear2 = 2.0 * sum(phase[a] * lame(1, a) for a in range(4))
    eig = [sum(phase[a] * eigen(a, p) for a in range(4)) for p in range(6)]
    return lam, shear2, eig


def stress_from(elastic, lam, shear2):
    trace = lam * (elastic[0] + elastic[1] + elastic[2])
    return [shear2 * elastic[p] + trace if p < 3 else shear2 * elastic[p] for p in range(6)]


def put_split(values, row, size, high_ref, low_ref):
    for i, p in enumerate(ORDER):
        high, low = split(values[p])
        high_ref[pl.ds(i * 128 + row, size), :] = high
        low_ref[pl.ds(i * 128 + row, size), :] = low


NT = ((1,), (1,))


def z_forward(tab_ref, high_ref, low_ref, send_ref):
    for which, (start, comps) in enumerate(((0, EVEN), (512, ODD))):
        rows = 128 * len(comps)
        high = high_ref[pl.ds(start, rows), :]
        low = low_ref[pl.ds(start, rows), :]
        t_high, t_low = tab_ref[2 * which], tab_ref[2 * which + 1]
        out = dot(t_high, high, NT) + dot(t_high, low, NT) + dot(t_low, high, NT)
        for i, c in enumerate(comps):
            r, k = divmod(c, 3)
            for par in range(2):
                for sh in range(8):
                    at = par * 64 + sh * 8
                    piece = out[at : at + 8, i * 128 : i * 128 + 128]
                    send_ref[pl.ds((sh * 16 + r * 8) * 6 + k * 2 + par, 8, stride=6), :] = piece


def z_inverse(tab_ref, recv_ref, c):
    r, k = divmod(c, 3)
    pieces = [
        recv_ref[pl.ds((sh * 16 + r * 8) * 6 + k * 2 + par, 8, stride=6), :] for par in range(2) for sh in range(8)
    ]
    data = jnp.concatenate(pieces, axis=0).T
    which = 4 + 2 * (c in ODD)
    t_high, t_low = tab_ref[which], tab_ref[which + 1]
    high, low = split(data)
    return dot(high, t_high) + dot(low, t_high) + dot(high, t_low)


def first_kernel(
    labels_hbm,
    noise_hbm,
    lame_hbm,
    eigen_hbm,
    tab_hbm,
    phase_ref,
    send_ref,
    par_ref,
    labels_ref,
    noise_ref,
    lame_ref,
    eigen_ref,
    tab_ref,
    high_ref,
    low_ref,
    sem,
):
    copies = [
        pltpu.make_async_copy(source, target, sem.at[i])
        for i, (source, target) in enumerate(
            (
                (lame_hbm, lame_ref),
                (eigen_hbm, eigen_ref),
                (labels_hbm, labels_ref),
                (noise_hbm, noise_ref),
                (tab_hbm, tab_ref),
            )
        )
    ]
    for copy in copies:
        copy.start()
    for copy in copies[:4]:
        copy.wait()
    write_params(lame_ref, eigen_ref, par_ref)

    def lame(i, a):
        return lame_ref[i, a]

    def eigen(a, p):
        return eigen_ref[a, p]

    for p in range(4):
        label = dense(labels_ref[p], labels_ref[p + 4])
        raw = [
            dense(noise_ref[a, p], noise_ref[a, p + 4]) + jnp.where(label == a, 2.0, 0.0).astype(F32)
            for a in range(4)
        ]
        inverse = 1.0 / (raw[0] + raw[1] + raw[2] + raw[3])
        phase = [raw[a] * inverse for a in range(4)]
        for a in range(4):
            phase_ref[a, pl.ds(p * 32, 32), :] = phase[a]
        lam, shear2, eig = material(phase, lame, eigen)
        stress = stress_from([-v for v in eig], lam, shear2)
        put_split(stress, p * 32, 32, high_ref, low_ref)
    copies[4].wait()
    z_forward(tab_ref, high_ref, low_ref, send_ref)


def middle_kernel(recv_ref, phase_ref, par_ref, tab_ref, strain_ref, send_ref, high_ref, low_ref):
    par = Params(par_ref)
    for c in range(6):
        strain_ref[c] = -z_inverse(tab_ref, recv_ref, c)
    for p in range(4):
        rows = pl.ds(p * 32, 32)
        phase = [phase_ref[a, rows, :] for a in range(4)]
        lam, shear2, eig = material(phase, par.lame, par.eigen)
        stress = stress_from([strain_ref[c, rows, :] - eig[c] for c in range(6)], lam, shear2)
        put_split(stress, p * 32, 32, high_ref, low_ref)
    z_forward(tab_ref, high_ref, low_ref, send_ref)


def last_kernel(
    recv_ref, phase_ref, strain_ref, force_ref, par_ref, tab_ref, next_hbm, stress_hbm, work_ref, next_ref, stress_ref, sem
):
    par = Params(par_ref)
    for c in range(6):
        work_ref[c] = strain_ref[c] - z_inverse(tab_ref, recv_ref, c)
    copies = []
    for p in range(4):
        rows = pl.ds(p * 32, 32)
        phase = [phase_ref[a, rows, :] for a in range(4)]
        lam, shear2, eig = material(phase, par.lame, par.eigen)
        elastic = [work_ref[c, rows, :] - eig[c] for c in range(6)]
        stress = stress_from(elastic, lam, shear2)
        for c in range(6):
            stress_ref[p, 0, c] = stress[c][:, :64]
            stress_ref[p, 1, c] = stress[c][:, 64:]
        trace = elastic[0] + elastic[1] + elastic[2]
        trace = 0.5 * trace * trace
        squares = (
            elastic[0] * elastic[0]
            + elastic[1] * elastic[1]
            + elastic[2] * elastic[2]
            + 2.0 * (elastic[3] * elastic[3] + elastic[4] * elastic[4] + elastic[5] * elastic[5])
        )
        doubled = [stress[c] if c < 3 else 2.0 * stress[c] for c in range(6)]
        force = []
        for a in range(4):
            coupling = sum(doubled[c] * par.eigen(a, c) for c in range(6))
            force.append(force_ref[a, rows, :] + par.lame(0, a) * trace + par.lame(1, a) * squares - coupling)
        mean = 0.25 * (force[0] + force[1] + force[2] + force[3])
        for a in range(4):
            new = phase[a] - STEP_PHASE * (force[a] - mean)
            next_ref[p, 0, a] = new[:, :64]
            next_ref[p, 1, a] = new[:, 64:]
        for half in range(2):
            x = p + 4 * half
            copies.append(pltpu.make_async_copy(stress_ref.at[p, half], stress_hbm.at[:, x], sem.at[2 * x]))
            copies.append(pltpu.make_async_copy(next_ref.at[p, half], next_hbm.at[:, x], sem.at[2 * x + 1]))
        for copy in copies[-4:]:
            copy.start()
    for copy in copies:
        copy.wait()


def swap_blocks(x):
    lane = lax.broadcasted_iota(jnp.int32, x[0].shape, 1)
    wide = lane < 64
    narrow = (lane & 32) == 0
    a = [jnp.where(wide, x[i], pltpu.roll(x[i + 2], 64, 1)) for i in range(2)]
    b = [jnp.where(wide, pltpu.roll(x[i], 64, 1), x[i + 2]) for i in range(2)]
    out = []
    for first, second in (a, b):
        out.append(jnp.where(narrow, first, pltpu.roll(second, 32, 1)))
        out.append(jnp.where(narrow, pltpu.roll(first, 96, 1), second))
    return out


def spectrum_kernel(recv_ref, xf_ref, y_ref, *refs):
    out_ref, high_ref, low_ref, mid_ref = refs[-4:]
    xf_high, xf_low = xf_ref[0], xf_ref[1]
    for k in range(3):
        rows = []
        for par in range(2):
            columns = []
            for gh in range(2):
                pieces = [
                    recv_ref[pl.ds((4 * gh + i) * 6 + k * 2 + par, 16, stride=48), :] for i in range(4)
                ]
                columns.append(swap_blocks(pieces))
            rows += [jnp.concatenate([columns[0][p], columns[1][p]], axis=1) for p in range(4)]
        high, low = split(jnp.concatenate(rows, axis=0))
        out = dot(xf_high, high) + dot(xf_high, low) + dot(xf_low, high)
        high, low = split(out)
        high_ref[pl.ds(k * 128, 128), :] = high
        low_ref[pl.ds(k * 128, 128), :] = low
    y_high, y_low = y_ref[0], y_ref[1]
    mid_ref[...] = dot(high_ref[...], y_high) + dot(low_ref[...], y_high) + dot(high_ref[...], y_low)
    for k in range(3):
        real, imag = pl.ds(k * 128, 64), pl.ds(k * 128 + 64, 64)
        out_ref[real, :] = mid_ref[real, :256] + mid_ref[imag, 256:]
        out_ref[imag, :] = mid_ref[imag, :256] - mid_ref[real, 256:]


def green_tile(re, im, wx, wy, omega, first, second, upper):
    xx, yy, zz, yz, xz, xy = range(6)
    vx = (re[xx] * wx + re[xy] * wy + omega * im[xz], im[xx] * wx + im[xy] * wy - omega * re[xz])
    vy = (re[xy] * wx + re[yy] * wy + omega * im[yz], im[xy] * wx + im[yy] * wy - omega * re[yz])
    vz = (re[xz] * wx + re[yz] * wy - omega * im[zz], im[xz] * wx + im[yz] * wy + omega * re[zz])
    inner = (wx * vx[0] + wy * vy[0] + omega * vz[1], wx * vx[1] + wy * vy[1] - omega * vz[0])
    s = [inner[part] * second for part in range(2)]
    fx = [vx[part] * first for part in range(2)]
    fy = [vy[part] * first for part in range(2)]
    fz = [vz[part] * first for part in range(2)]
    out = []
    for part in range(2):
        other = 1 - part
        if upper:
            sign = -omega if part == 0 else omega
            out.append(
                (
                    wy * fz[part] + sign * (fy[other] - wy * s[other]),
                    wx * fz[part] + sign * (fx[other] - wx * s[other]),
                    wx * (fy[part] - wy * s[part]) + wy * fx[part],
                )
            )
        else:
            turned = fz[1] if part == 0 else -fz[0]
            out.append(
                (
                    wx * (2.0 * fx[part] - wx * s[part]),
                    wy * (2.0 * fy[part] - wy * s[part]),
                    omega * (2.0 * turned - omega * s[part]),
                )
            )
    return out


def green_kernel(own_ref, other_ref, after_ref, par_ref, xi_ref, y_ref, send_ref, high_ref, low_ref, mid_ref):
    del after_ref
    x_index, y_index = lax.axis_index("gx"), lax.axis_index("gy")
    core = lax.rem(x_index, 2)
    slab = lax.div(x_index, 2) * 8 + y_index
    omega = jnp.where(slab < 32, slab, 32 - slab).astype(F32) * (1.0 / 64.0)
    par = Params(par_ref)
    lam0 = jnp.concatenate([par.row(32), par.row(32)], axis=1)
    mu0 = jnp.concatenate([par.row(33), par.row(33)], axis=1)
    half_mu = 0.5 / mu0
    ratio = (lam0 + mu0) / (mu0 * (lam0 + 2.0 * mu0))
    lane = lax.broadcasted_iota(jnp.int32, (8, 256), 1)
    index = jnp.where(lane >= 128, lane - 256, lane)
    wy = jnp.where(lane == 128, 0, index).astype(F32) * (1.0 / 256.0)
    row = lax.broadcasted_iota(jnp.int32, (8, 256), 0)

    def green(upper):
        for tile in range(8):
            wx = (row + tile * 8).astype(F32) * (1.0 / 128.0)
            q = wx * wx + wy * wy + omega * omega
            inverse = 1.0 / jnp.where(q == 0.0, 1.0, q)
            first = half_mu * inverse
            second = ratio * inverse * inverse

            def get(ref, part):
                return [ref[pl.ds(k * 128 + part * 64 + tile * 8, 8), :] for k in range(3)]

            low, high = (other_ref, own_ref) if upper else (own_ref, other_ref)
            re, im = (get(low, part) + get(high, part) for part in range(2))
            out = green_tile(re, im, wx, wy, omega, first, second, upper)
            for part in range(2):
                for k in range(3):
                    high, low = split(out[part][k])
                    at = pl.ds(k * 128 + part * 64 + tile * 8, 8)
                    high_ref[at, :] = high
                    low_ref[at, :] = low

    @pl.when(core == 0)
    def _():
        green(False)

    @pl.when(core == 1)
    def _():
        green(True)

    y_high, y_low = y_ref[0], y_ref[1]
    mid_ref[...] = dot(high_ref[...], y_high) + dot(low_ref[...], y_high) + dot(high_ref[...], y_low)
    xi_high, xi_low = xi_ref[0], xi_ref[1]
    for k in range(3):
        r_rows, i_rows = pl.ds(k * 128, 64), pl.ds(k * 128 + 64, 64)
        real = mid_ref[r_rows, :256] - mid_ref[i_rows, 256:]
        imag = mid_ref[i_rows, :256] + mid_ref[r_rows, 256:]
        high, low = split(jnp.concatenate([real, imag], axis=0))
        out = dot(xi_high, high) + dot(xi_high, low) + dot(xi_low, high)
        for parity in range(2):
            for gh in range(2):
                lanes = slice(gh * 128, gh * 128 + 128)
                pieces = [out[parity * 64 + p * 16 : parity * 64 + p * 16 + 16, lanes] for p in range(4)]
                for i, value in enumerate(swap_blocks(pieces)):
                    send_ref[pl.ds((4 * gh + i) * 6 + k * 2 + parity, 16, stride=48), :] = value


def newton_kernel(
    conc_ref,
    phase_ref,
    curvature,
    quartic,
    wells,
    after_ref,
    chem_ref,
    chemical_ref,
    xlow_ref,
    xhigh_ref,
    ylow_ref,
    yhigh_ref,
):
    del after_ref
    for p in range(4):
        rows = pl.ds(p * 32, 32)
        conc = dense(conc_ref[p], conc_ref[p + 4])
        phase = [phase_ref[a, rows, :] for a in range(4)]
        part = [conc] * 4
        chem = jnp.zeros_like(conc)
        for a in range(4):
            dev = conc - wells[a]
            chem = chem + phase[a] * (dev * (curvature[a] + quartic[a] * dev * dev))
        for _ in range(NEWTON):
            top = conc
            bottom = jnp.zeros_like(conc)
            slope, recip = [], []
            for a in range(4):
                dev = part[a] - wells[a]
                square = quartic[a] * dev * dev
                g = dev * (curvature[a] + square) - chem
                d = 1.0 / (curvature[a] + 3.0 * square)
                slope.append(g)
                recip.append(d)
                top = top + phase[a] * (g * d - part[a])
                bottom = bottom + phase[a] * d
            shift = top / bottom
            part = [part[a] + (shift - slope[a]) * recip[a] for a in range(4)]
            chem = chem + shift
        chem_ref[rows, :] = chem
        total = sum(phase[a] * phase[a] for a in range(4))
        for a in range(4):
            dev = part[a] - wells[a]
            square = dev * dev
            energy = square * (0.5 * curvature[a] + 0.25 * quartic[a] * square)
            chemical_ref[a, rows, :] = energy - chem * part[a] + 2.0 * phase[a] * (total - phase[a] * phase[a])
    low_half = lax.broadcasted_iota(jnp.int32, (32, 128), 1) < 64

    def field(f, rows):
        return phase_ref[f, rows, :] if f < 4 else chem_ref[rows, :]

    first, last = pl.ds(0, 32), pl.ds(96, 32)
    for j in range(2):
        at = pl.ds(j * 32, 32)
        xlow_ref[at, :] = jnp.where(low_half, field(2 * j, first), pltpu.roll(field(2 * j + 1, first), 64, 1))
        xhigh_ref[at, :] = jnp.where(low_half, pltpu.roll(field(2 * j, last), 64, 1), field(2 * j + 1, last))
    xlow_ref[pl.ds(64, 32), :] = field(4, first)
    xhigh_ref[pl.ds(64, 32), :] = pltpu.roll(field(4, last), 64, 1)
    for f in range(5):
        for p in range(4):
            ylow_ref[pl.ds(f * 4 + p, 1), :] = field(f, pl.ds(p * 32, 1))
            yhigh_ref[pl.ds(f * 4 + p, 1), :] = field(f, pl.ds(p * 32 + 31, 1))
    pad = jnp.zeros((4, 128), F32)
    ylow_ref[pl.ds(20, 4), :] = pad
    yhigh_ref[pl.ds(20, 4), :] = pad


def laplace_kernel(
    phase_ref,
    chem_ref,
    chemical_ref,
    conc_ref,
    xlow_ref,
    xhigh_ref,
    ylow_ref,
    yhigh_ref,
    after_ref,
    force_ref,
    conc_out_ref,
):
    del after_ref
    lane = lax.broadcasted_iota(jnp.int32, (32, 128), 1)
    row = lax.broadcasted_iota(jnp.int32, (32, 128), 0)
    first_z = (lane & 63) == 0
    last_z = (lane & 63) == 63
    low_half = lane < 64
    for f in range(5):
        block = [phase_ref[f, pl.ds(p * 32, 32), :] if f < 4 else chem_ref[pl.ds(p * 32, 32), :] for p in range(4)]
        at = pl.ds(f // 2 * 32, 32)
        before, after = xlow_ref[at, :], xhigh_ref[at, :]
        if f % 2 == 0:
            after = pltpu.roll(after, 64, 1)
        else:
            before = pltpu.roll(before, 64, 1)
        for p in range(4):
            here = block[p]
            total = -6.0 * here
            if p > 0:
                total = total + block[p - 1]
            else:
                total = total + jnp.where(low_half, before, pltpu.roll(block[3], 64, 1))
            if p < 3:
                total = total + block[p + 1]
            else:
                total = total + jnp.where(low_half, pltpu.roll(block[0], 64, 1), after)
            y_before = ylow_ref[pl.ds(f * 4 + p, 1), :]
            y_after = yhigh_ref[pl.ds(f * 4 + p, 1), :]
            total = total + jnp.where(row == 0, y_before, pltpu.roll(here, 1, 0))
            total = total + jnp.where(row == 31, y_after, pltpu.roll(here, 31, 0))
            total = total + jnp.where(first_z, pltpu.roll(here, 65, 1), pltpu.roll(here, 1, 1))
            total = total + jnp.where(last_z, pltpu.roll(here, 63, 1), pltpu.roll(here, 127, 1))
            if f < 4:
                rows = pl.ds(p * 32, 32)
                force_ref[f, rows, :] = chemical_ref[f, rows, :] - total
            else:
                conc_out_ref[p] = conc_ref[p] + STEP_CONC * total[:, :64]
                conc_out_ref[p + 4] = conc_ref[p + 4] + STEP_CONC * total[:, 64:]


VMEM = pl.BlockSpec(memory_space=pltpu.VMEM)
SMEM = pl.BlockSpec(memory_space=pltpu.SMEM)
HBM = pl.BlockSpec(memory_space=pltpu.HBM)
ANY = pl.BlockSpec(memory_space=pl.ANY)
LIMIT = 12 * 1024 * 1024


def call(kernel, args, out, scratch=(), special=None, out_spec=VMEM, cost=4e6):
    special = special or {}
    specs = [special.get(i, VMEM) for i in range(len(args))]
    shapes = [jax.ShapeDtypeStruct(s, F32) for s in out]
    return pl.pallas_call(
        kernel,
        out_shape=shapes,
        in_specs=specs,
        out_specs=[out_spec] * len(out),
        scratch_shapes=list(scratch),
        compiler_params=pltpu.CompilerParams(vmem_limit_bytes=LIMIT),
        cost_estimate=pl.CostEstimate(flops=int(cost), bytes_accessed=int(cost), transcendentals=0),
    )(*args)


def exchange(x):
    y = lax.all_to_all(x.reshape(128, 1, 768), BOTH, 0, 0, tiled=True)
    return y.reshape(768, 128)


def step(labels, seed_noise, conc, curvature, quartic, wells, lame, eigen):
    tables = [half for t in z_tables() for half in split_np(t)]
    z_tab = jnp.asarray(np.stack(tables))
    x_forward, x_inverse = x_tables()
    xf = jnp.asarray(np.stack(split_np(x_forward)))
    xi = jnp.asarray(np.stack(split_np(x_inverse)))
    yt = jnp.asarray(np.stack(split_np(y_table())))

    halves = [pltpu.VMEM((768, 128), BF16), pltpu.VMEM((768, 128), BF16)]
    plane_scratch = [
        pltpu.VMEM((384, 256), BF16),
        pltpu.VMEM((384, 256), BF16),
        pltpu.VMEM((384, 512), F32),
    ]

    def shift(value, axis, step):
        count = lax.axis_size(axis)
        return lax.ppermute(value, axis, [(i, (i + step) % count) for i in range(count)])

    def spectrum(recv, after):
        (own,) = call(
            spectrum_kernel,
            (recv, xf, yt, *after),
            [(384, 256)],
            plane_scratch,
            {3 + i: ANY for i in range(len(after))},
        )
        return own, lax.ppermute(own, "gx", [(i, i ^ 1) for i in range(16)])

    def update(own, other, after, par):
        (back,) = call(green_kernel, (own, other, after, par, xi, yt), [(768, 128)], plane_scratch, {2: ANY})
        return exchange(back)

    def in_hbm(*arrays):
        return tuple(pltpu.with_memory_space_constraint(a, pltpu.HBM) for a in arrays)

    phase, send, par = call(
        first_kernel,
        in_hbm(labels, seed_noise, lame, eigen, z_tab),
        [(4, 128, 128), (768, 128), (40, 128)],
        [
            pltpu.VMEM((8, 32, 64), jnp.int32),
            pltpu.VMEM((4, 8, 32, 64), F32),
            pltpu.SMEM((2, 4), F32),
            pltpu.SMEM((4, 6), F32),
            pltpu.VMEM((8, 128, 128), BF16),
            *halves,
            pltpu.SemaphoreType.DMA((5,)),
        ],
        {i: HBM for i in range(5)},
    )
    recv = exchange(send)

    own, other = spectrum(recv, ())
    chem, chemical, xlow, xhigh, ylow, yhigh = call(
        newton_kernel,
        (conc, phase, curvature, quartic, wells, own),
        [(128, 128), (4, 128, 128), (96, 128), (96, 128), (24, 128), (24, 128)],
        special={2: SMEM, 3: SMEM, 4: SMEM, 5: ANY},
    )
    halo = [shift(xhigh, "gx", 1), shift(xlow, "gx", -1), shift(yhigh, "gy", 1), shift(ylow, "gy", -1)]
    back = update(own, other, ylow, par)
    strain, send = call(middle_kernel, (back, phase, par, z_tab), [(6, 128, 128), (768, 128)], halves)
    own, other = spectrum(exchange(send), ())
    force, conc_next = call(
        laplace_kernel, (phase, chem, chemical, conc, *halo, own), [(4, 128, 128), (8, 32, 64)], special={8: ANY}
    )
    back = update(own, other, force, par)
    phase_next, stress = call(
        last_kernel,
        (back, phase, strain, force, par, z_tab),
        [(4, 8, 32, 64), (6, 8, 32, 64)],
        [
            pltpu.VMEM((6, 128, 128), F32),
            pltpu.VMEM((4, 2, 4, 32, 64), F32),
            pltpu.VMEM((4, 2, 6, 32, 64), F32),
            pltpu.SemaphoreType.DMA((16,)),
        ],
        out_spec=HBM,
    )
    return (phase_next, conc_next, stress)


def solution(mesh):
    in_specs = (
        P("gx", "gy", None),
        P(None, "gx", "gy", None),
        P("gx", "gy", None),
        P(),
        P(),
        P(),
        P(),
        P(),
    )
    out_specs = (P(None, "gx", "gy", None), P("gx", "gy", None), P(None, "gx", "gy", None))
    return jax.shard_map(step, mesh=mesh, in_specs=in_specs, out_specs=out_specs, check_vma=False)
```

```python
import numpy as np

import jax
import jax.numpy as jnp
from jax import lax
from jax.experimental import pallas as pl
from jax.experimental.pallas import tpu as pltpu
from jax.sharding import PartitionSpec as P


NEWTON = 5
STEP_PHASE = 0.06
STEP_CONC = 0.005

F32 = jnp.float32
BF16 = jnp.bfloat16

EVEN = (0, 1, 2, 5)
ODD = (3, 4)
ORDER = EVEN + ODD
BOTH = ("gy", "gx")


def split_np(table):
    high = table.astype(np.float32).astype(BF16)
    low = (table - high.astype(np.float64)).astype(np.float32).astype(BF16)
    return high, low


def stack_k(table, axis):
    high, low = split_np(table)
    return np.concatenate([high, high, low], axis=axis)


def z_tables():
    slab = np.arange(64)[:, None]
    z = np.arange(64)[None, :]
    freq = np.where(slab <= 32, slab, slab - 32)
    angle = 2.0 * np.pi * ((freq * z) % 64) / 64.0
    cos, sin = np.cos(angle), np.sin(angle)
    edge = (slab == 0) | (slab == 32)
    first = slab < 32
    even = np.where(edge | first, cos, sin)
    odd = np.where(edge | ~first, cos, sin)
    weight = np.where(edge, 1.0, 2.0) / 64.0

    def double(t):
        return np.kron(np.eye(2), t)

    forward = np.stack([stack_k(double(t), 1) for t in (even, odd)])
    inverse = np.stack([stack_k(double(t * weight), 0) for t in (even, odd)])
    return forward, inverse


def x_tables():
    order = np.array([8 * g + 4 * par + p for par in range(2) for p in range(4) for g in range(8)])
    forward, inverse = [], []
    for parity in range(2):
        k = 2 * np.arange(32)[:, None] + parity
        angle = 2.0 * np.pi * ((k * order[None, :]) % 128) / 128.0
        real, imag = np.cos(angle), -np.sin(angle)
        weight = np.full((64, 1), 2.0)
        if parity == 0:
            imag[0] = np.where(order % 2 == 0, 1.0, -1.0)
            weight[0] = weight[32] = 1.0
        table = np.concatenate([real, imag], axis=0)
        forward.append(stack_k(table, 1))
        inverse.append(stack_k((table * weight / (128.0 * 256.0)).T, 1))
    return np.stack(forward), np.stack(inverse)


def y_tables():
    y = np.arange(128)[:, None]
    m = np.arange(128)[None, :]
    tables = []
    for k, n in ((2 * m, y), (2 * m + 1, y), (2 * y + 1, m)):
        angle = 2.0 * np.pi * ((k * n) % 256) / 256.0
        tables.append(stack_k(np.concatenate([np.cos(angle), np.sin(angle)], axis=1), 0))
    return np.stack(tables)


def split(value):
    high = value.astype(BF16)
    low = (value - high.astype(F32)).astype(BF16)
    return high, low


def dot(a, b, dims=((1,), (0,))):
    return lax.dot_general(a, b, (dims, ((), ())), preferred_element_type=F32)


def dense(low, high):
    return jnp.concatenate([low, high], axis=-1)


class Params:
    def __init__(self, ref):
        self.ref = ref

    def row(self, i):
        return self.ref[pl.ds(i, 1), :]

    def lame(self, i, a):
        return self.row(4 * i + a)

    def eigen(self, a, p):
        return self.row(8 + 6 * a + p)


def write_params(lame, eigen, others, ref):
    def middle(v):
        top = jnp.maximum(jnp.maximum(v[0], v[1]), jnp.maximum(v[2], v[3]))
        least = jnp.minimum(jnp.minimum(v[0], v[1]), jnp.minimum(v[2], v[3]))
        return 0.5 * (top + least)

    values = [lame[i, a] for i in range(2) for a in range(4)]
    values += [eigen[a, p] for a in range(4) for p in range(6)]
    values += [middle(values[0:4]), middle(values[4:8])]
    values += [v[a] for v in others for a in range(4)]
    for i, value in enumerate(values):
        ref[pl.ds(i, 1), :] = jnp.full((1, 128), value, F32)


def material(phase, lame, eigen):
    lam = sum(phase[a] * lame(0, a) for a in range(4))
    shear2 = 2.0 * sum(phase[a] * lame(1, a) for a in range(4))
    eig = [sum(phase[a] * eigen(a, p) for a in range(4)) for p in range(6)]
    return lam, shear2, eig


def stress_from(elastic, lam, shear2):
    trace = lam * (elastic[0] + elastic[1] + elastic[2])
    return [shear2 * elastic[p] + trace if p < 3 else shear2 * elastic[p] for p in range(6)]


def cell_block(b):
    return lax.rem(b + 4 - lax.rem(lax.axis_index("gy"), 4), 4)


def block_rows(p):
    return pl.ds(pl.multiple_of(p * 32, 32), 32)


def put_split(values, b, data_ref):
    for i, c in enumerate(ORDER):
        high, low = split(values[c])
        at = pl.ds(pl.multiple_of(i * 128 + b * 32, 32), 32)
        data_ref[at, :128] = high
        data_ref[at, 128:] = low


NT = ((1,), (1,))


def stack3(value, axis):
    high, low = split(value)
    return jnp.concatenate([high, low, high], axis=axis)


def z_forward(tab_ref, data_ref, send_ref):
    for which, (start, comps) in enumerate(((0, EVEN), (512, ODD))):
        data = data_ref[pl.ds(start, 128 * len(comps)), :]
        out = dot(tab_ref[which], jnp.concatenate([data, data[:, :128]], axis=1), NT)
        for i, c in enumerate(comps):
            r, k = divmod(c, 3)
            for par in range(2):
                piece = out[par * 64 : par * 64 + 64, i * 128 : i * 128 + 128]
                send_ref[pl.ds(r * 6 + k * 2 + par, 64, stride=12), :] = piece


def z_inverse(tab_ref, recv_ref, c):
    r, k = divmod(c, 3)
    pieces = [recv_ref[pl.ds(r * 6 + k * 2 + par, 64, stride=12), :] for par in range(2)]
    data = jnp.concatenate(pieces, axis=0).T
    return dot(stack3(data, 1), tab_ref[int(c in ODD)])


def first_kernel(*refs):
    sources, (phase_ref, mat_ref, send_ref, par_ref), targets, (data_ref, sem) = refs[:8], refs[8:12], refs[12:20], refs[20:]
    copies = [pltpu.make_async_copy(a, b, sem.at[i]) for i, (a, b) in enumerate(zip(sources, targets))]
    for copy in copies:
        copy.start()
    labels_ref, noise_ref, lame_ref, eigen_ref, *others, tab_ref = targets
    for copy in copies[:4]:
        copy.wait()
    by = lax.rem(lax.axis_index("gy"), 4)

    def lame(i, a):
        return lame_ref[i, a]

    def eigen(a, p):
        return eigen_ref[a, p]

    for p in range(4):
        rows = pl.ds(p * 32, 32)
        label = dense(labels_ref[p], labels_ref[p + 4])
        raw = [
            dense(noise_ref[a, p], noise_ref[a, p + 4]) + jnp.where(label == a, 2.0, 0.0).astype(F32)
            for a in range(4)
        ]
        inverse = 1.0 / (raw[0] + raw[1] + raw[2] + raw[3])
        phase = [raw[a] * inverse for a in range(4)]
        for a in range(4):
            phase_ref[a, rows, :] = phase[a]
        lam, shear2, eig = material(phase, lame, eigen)
        for i, value in enumerate([lam, shear2, *eig]):
            mat_ref[i, rows, :] = value
        put_split(stress_from([-v for v in eig], lam, shear2), lax.rem(p + by, 4), data_ref)
    for copy in copies[4:]:
        copy.wait()
    z_forward(tab_ref, data_ref, send_ref)
    write_params(lame_ref, eigen_ref, others, par_ref)


def middle_kernel(recv_ref, mat_ref, tab_ref, inv_ref, strain_ref, send_ref, data_ref):
    strain = []
    for c in range(6):
        strain.append(-z_inverse(inv_ref, recv_ref, c))
        strain_ref[c] = strain[c]
    for b in range(4):
        rows = block_rows(cell_block(b))
        lam, shear2, *eig = [mat_ref[i, rows, :] for i in range(8)]
        elastic = [strain[c][b * 32 : b * 32 + 32] - eig[c] for c in range(6)]
        put_split(stress_from(elastic, lam, shear2), b, data_ref)
    z_forward(tab_ref, data_ref, send_ref)


def last_kernel(
    recv_ref,
    phase_ref,
    mat_ref,
    strain_ref,
    force_ref,
    par_ref,
    inv_ref,
    next_hbm,
    stress_hbm,
    next_ref,
    stress_ref,
    sem,
):
    par = Params(par_ref)
    strain = [strain_ref[c] - z_inverse(inv_ref, recv_ref, c) for c in range(6)]
    copies = []
    for b in range(4):
        p = cell_block(b)
        rows = block_rows(p)
        lam, shear2, *eig = [mat_ref[i, rows, :] for i in range(8)]
        elastic = [strain[c][b * 32 : b * 32 + 32] - eig[c] for c in range(6)]
        stress = stress_from(elastic, lam, shear2)
        for c in range(6):
            stress_ref[b, 0, c] = stress[c][:, :64]
            stress_ref[b, 1, c] = stress[c][:, 64:]
        for half in range(2):
            x = p + 4 * half
            at = 4 * b + 2 * half
            copies.append(pltpu.make_async_copy(stress_ref.at[b, half], stress_hbm.at[:, x], sem.at[at]))
            copies[-1].start()
        trace = elastic[0] + elastic[1] + elastic[2]
        trace = 0.5 * trace * trace
        squares = (
            elastic[0] * elastic[0]
            + elastic[1] * elastic[1]
            + elastic[2] * elastic[2]
            + 2.0 * (elastic[3] * elastic[3] + elastic[4] * elastic[4] + elastic[5] * elastic[5])
        )
        doubled = [stress[c] if c < 3 else 2.0 * stress[c] for c in range(6)]
        force = []
        for a in range(4):
            coupling = sum(doubled[c] * par.eigen(a, c) for c in range(6))
            force.append(force_ref[a, rows, :] + par.lame(0, a) * trace + par.lame(1, a) * squares - coupling)
        mean = 0.25 * (force[0] + force[1] + force[2] + force[3])
        for a in range(4):
            new = phase_ref[a, rows, :] - STEP_PHASE * (force[a] - mean)
            next_ref[b, 0, a] = new[:, :64]
            next_ref[b, 1, a] = new[:, 64:]
        for half in range(2):
            x = p + 4 * half
            at = 4 * b + 2 * half + 1
            copies.append(pltpu.make_async_copy(next_ref.at[b, half], next_hbm.at[:, x], sem.at[at]))
            copies[-1].start()
    for copy in copies:
        copy.wait()


def mix(x):
    lane = lax.broadcasted_iota(jnp.int32, x[0].shape, 1)
    low = lane < 64
    even = (lane & 32) == 0
    e01, e23, e30, e12 = (jnp.where(even, x[a], x[b]) for a, b in ((0, 1), (2, 3), (3, 0), (1, 2)))
    return [jnp.where(low, a, b) for a, b in ((e01, e23), (e30, e12), (e23, e01), (e12, e30))]


def roll_lanes(x, by):
    return pltpu.roll(x, by, 1) if by else x


def spectrum_kernel(recv_ref, xf_ref, y_ref, *refs):
    out_ref, even_ref, odd_ref = refs[-3:]
    for k in range(3):
        total, delta = [], []
        for par in range(2):
            columns = []
            for gh in range(2):
                pieces = [recv_ref[pl.ds((4 * gh + i) * 96 + k * 2 + par, 16, stride=6), :] for i in range(4)]
                columns.append([roll_lanes(v, (128 - 32 * p) % 128) for p, v in enumerate(mix(pieces))])
            for p in range(4):
                both = jnp.concatenate([columns[0][p], columns[1][p]], axis=1)
                total.append(both[:8] + both[8:])
                delta.append(both[:8] - both[8:])
        even = dot(xf_ref[0], stack3(jnp.concatenate(total, axis=0), 0))
        odd = dot(xf_ref[1], stack3(jnp.concatenate(delta, axis=0), 0))
        value = jnp.concatenate([even[:32], odd[:32], even[32:], odd[32:]], axis=0)
        left, right = value[:, :128], value[:, 128:]
        rows = pl.ds(k * 128, 128)
        even_ref[rows, :] = stack3(left + right, 1)
        odd_ref[rows, :] = stack3(left - right, 1)
    for which, ref in enumerate((even_ref, odd_ref)):
        mid = dot(ref[...], y_ref[which])
        lanes = slice(which * 128, which * 128 + 128)
        for k in range(3):
            real, imag = mid[k * 128 : k * 128 + 64], mid[k * 128 + 64 : k * 128 + 128]
            out_ref[pl.ds(k * 128, 64), lanes] = real[:, :128] + imag[:, 128:]
            out_ref[pl.ds(k * 128 + 64, 64), lanes] = imag[:, :128] - real[:, 128:]


def green_tile(re, im, wx, wy, omega, first, second, upper):
    xx, yy, zz, yz, xz, xy = range(6)
    vx = (re[xx] * wx + re[xy] * wy + omega * im[xz], im[xx] * wx + im[xy] * wy - omega * re[xz])
    vy = (re[xy] * wx + re[yy] * wy + omega * im[yz], im[xy] * wx + im[yy] * wy - omega * re[yz])
    vz = (re[xz] * wx + re[yz] * wy - omega * im[zz], im[xz] * wx + im[yz] * wy + omega * re[zz])
    inner = (wx * vx[0] + wy * vy[0] + omega * vz[1], wx * vx[1] + wy * vy[1] - omega * vz[0])
    s = [inner[part] * second for part in range(2)]
    fx = [vx[part] * first for part in range(2)]
    fy = [vy[part] * first for part in range(2)]
    fz = [vz[part] * first for part in range(2)]
    out = []
    for part in range(2):
        other = 1 - part
        if upper:
            sign = -omega if part == 0 else omega
            out.append(
                (
                    wy * fz[part] + sign * (fy[other] - wy * s[other]),
                    wx * fz[part] + sign * (fx[other] - wx * s[other]),
                    wx * (fy[part] - wy * s[part]) + wy * fx[part],
                )
            )
        else:
            turned = fz[1] if part == 0 else -fz[0]
            out.append(
                (
                    wx * (2.0 * fx[part] - wx * s[part]),
                    wy * (2.0 * fy[part] - wy * s[part]),
                    omega * (2.0 * turned - omega * s[part]),
                )
            )
    return out


def green_kernel(own_ref, other_ref, after_ref, par_ref, xi_ref, y_ref, send_ref, even_ref, odd_ref):
    del after_ref
    x_index, y_index = lax.axis_index("gx"), lax.axis_index("gy")
    core = lax.rem(x_index, 2)
    slab = y_index * 8 + lax.div(x_index, 2)
    omega = jnp.where(slab < 32, slab, 32 - slab).astype(F32) * (1.0 / 64.0)
    par = Params(par_ref)
    lam0 = jnp.concatenate([par.row(32), par.row(32)], axis=1)
    mu0 = jnp.concatenate([par.row(33), par.row(33)], axis=1)
    half_mu = 0.5 / mu0
    ratio = (lam0 + mu0) / (mu0 * (lam0 + 2.0 * mu0))
    lane = lax.broadcasted_iota(jnp.int32, (8, 256), 1)
    index = jnp.where(lane < 128, 2 * lane, 2 * lane - 255)
    index = jnp.where(index == 128, 0, jnp.where(index > 128, index - 256, index))
    wy = index.astype(F32) * (1.0 / 256.0)
    row = lax.broadcasted_iota(jnp.int32, (8, 256), 0)

    def green(upper):
        for tile in range(8):
            wx = (2 * row + (tile % 4 * 16 + tile // 4)).astype(F32) * (1.0 / 128.0)
            q = wx * wx + wy * wy + omega * omega
            inverse = 1.0 / jnp.where(q == 0.0, 1.0, q)
            first = half_mu * inverse
            second = ratio * inverse * inverse

            def get(ref, part):
                return [ref[pl.ds(k * 128 + part * 64 + tile * 8, 8), :] for k in range(3)]

            low, high = (other_ref, own_ref) if upper else (own_ref, other_ref)
            re, im = (get(low, part) + get(high, part) for part in range(2))
            out = green_tile(re, im, wx, wy, omega, first, second, upper)
            for part in range(2):
                for k in range(3):
                    at = pl.ds(k * 128 + part * 64 + tile * 8, 8)
                    value = stack3(out[part][k], 0)
                    for i in range(3):
                        piece = value[i * 8 : i * 8 + 8]
                        even_ref[at, i * 128 : i * 128 + 128] = piece[:, :128]
                        odd_ref[at, i * 128 : i * 128 + 128] = piece[:, 128:]

    @pl.when(core == 0)
    def _():
        green(False)

    @pl.when(core == 1)
    def _():
        green(True)

    halves = []
    for ref, table in ((even_ref, y_ref[0]), (odd_ref, y_ref[2])):
        halves.append(dot(ref[...], table))
    for k in range(3):
        sums = []
        for mid in halves:
            real, imag = mid[k * 128 : k * 128 + 64], mid[k * 128 + 64 : k * 128 + 128]
            sums.append((real[:, :128] - imag[:, 128:], imag[:, :128] + real[:, 128:]))
        (re_e, im_e), (re_o, im_o) = sums
        real = jnp.concatenate([re_e + re_o, re_e - re_o], axis=1)
        imag = jnp.concatenate([im_e + im_o, im_e - im_o], axis=1)
        even = dot(xi_ref[0], stack3(jnp.concatenate([real[:32], imag[:32]], axis=0), 0))
        odd = dot(xi_ref[1], stack3(jnp.concatenate([real[32:], imag[32:]], axis=0), 0))
        total, delta = even + odd, even - odd
        for parity in range(2):
            for gh in range(2):
                lanes = slice(gh * 128, gh * 128 + 128)
                pieces = []
                for p in range(4):
                    rows = slice(parity * 32 + p * 8, parity * 32 + p * 8 + 8)
                    pieces.append(
                        roll_lanes(jnp.concatenate([total[rows, lanes], delta[rows, lanes]], axis=0), 32 * p)
                    )
                for i, value in enumerate(mix(pieces)):
                    send_ref[pl.ds((4 * gh + i) * 96 + k * 2 + parity, 16, stride=6), :] = value


def newton_kernel(
    conc_ref,
    phase_ref,
    par_ref,
    after_ref,
    chem_ref,
    chemical_ref,
    xlow_ref,
    xhigh_ref,
    ylow_ref,
    yhigh_ref,
):
    del after_ref
    par = Params(par_ref)
    curvature, quartic, wells = ([par.row(34 + 4 * i + a) for a in range(4)] for i in range(3))
    for p in range(4):
        rows = pl.ds(p * 32, 32)
        conc = dense(conc_ref[p], conc_ref[p + 4])
        phase = [phase_ref[a, rows, :] for a in range(4)]
        part = [conc] * 4
        chem = jnp.zeros_like(conc)
        for a in range(4):
            dev = conc - wells[a]
            chem = chem + phase[a] * (dev * (curvature[a] + quartic[a] * dev * dev))
        for _ in range(NEWTON):
            top = conc
            bottom = jnp.zeros_like(conc)
            slope, recip = [], []
            for a in range(4):
                dev = part[a] - wells[a]
                square = quartic[a] * dev * dev
                g = dev * (curvature[a] + square) - chem
                d = 1.0 / (curvature[a] + 3.0 * square)
                slope.append(g)
                recip.append(d)
                top = top + phase[a] * (g * d - part[a])
                bottom = bottom + phase[a] * d
            shift = top / bottom
            part = [part[a] + (shift - slope[a]) * recip[a] for a in range(4)]
            chem = chem + shift
        chem_ref[rows, :] = chem
        total = sum(phase[a] * phase[a] for a in range(4))
        for a in range(4):
            dev = part[a] - wells[a]
            square = dev * dev
            energy = square * (0.5 * curvature[a] + 0.25 * quartic[a] * square)
            chemical_ref[a, rows, :] = energy - chem * part[a] + 2.0 * phase[a] * (total - phase[a] * phase[a])
    low_half = lax.broadcasted_iota(jnp.int32, (32, 128), 1) < 64

    def field(f, rows):
        return phase_ref[f, rows, :] if f < 4 else chem_ref[rows, :]

    first, last = pl.ds(0, 32), pl.ds(96, 32)
    for j in range(2):
        at = pl.ds(j * 32, 32)
        xlow_ref[at, :] = jnp.where(low_half, field(2 * j, first), pltpu.roll(field(2 * j + 1, first), 64, 1))
        xhigh_ref[at, :] = jnp.where(low_half, pltpu.roll(field(2 * j, last), 64, 1), field(2 * j + 1, last))
    xlow_ref[pl.ds(64, 32), :] = field(4, first)
    xhigh_ref[pl.ds(64, 32), :] = pltpu.roll(field(4, last), 64, 1)
    for f in range(5):
        for p in range(4):
            ylow_ref[pl.ds(f * 4 + p, 1), :] = field(f, pl.ds(p * 32, 1))
            yhigh_ref[pl.ds(f * 4 + p, 1), :] = field(f, pl.ds(p * 32 + 31, 1))
    pad = jnp.zeros((4, 128), F32)
    ylow_ref[pl.ds(20, 4), :] = pad
    yhigh_ref[pl.ds(20, 4), :] = pad


def laplace_kernel(
    phase_ref,
    chem_ref,
    chemical_ref,
    conc_ref,
    xlow_ref,
    xhigh_ref,
    ylow_ref,
    yhigh_ref,
    after_ref,
    force_ref,
    conc_out_ref,
):
    del after_ref
    lane = lax.broadcasted_iota(jnp.int32, (32, 128), 1)
    row = lax.broadcasted_iota(jnp.int32, (32, 128), 0)
    first_z = (lane & 63) == 0
    last_z = (lane & 63) == 63
    low_half = lane < 64
    for f in range(5):
        block = [phase_ref[f, pl.ds(p * 32, 32), :] if f < 4 else chem_ref[pl.ds(p * 32, 32), :] for p in range(4)]
        at = pl.ds(f // 2 * 32, 32)
        before, after = xlow_ref[at, :], xhigh_ref[at, :]
        if f % 2 == 0:
            after = pltpu.roll(after, 64, 1)
        else:
            before = pltpu.roll(before, 64, 1)
        for p in range(4):
            here = block[p]
            total = -6.0 * here
            if p > 0:
                total = total + block[p - 1]
            else:
                total = total + jnp.where(low_half, before, pltpu.roll(block[3], 64, 1))
            if p < 3:
                total = total + block[p + 1]
            else:
                total = total + jnp.where(low_half, pltpu.roll(block[0], 64, 1), after)
            y_before = ylow_ref[pl.ds(f * 4 + p, 1), :]
            y_after = yhigh_ref[pl.ds(f * 4 + p, 1), :]
            total = total + jnp.where(row == 0, y_before, pltpu.roll(here, 1, 0))
            total = total + jnp.where(row == 31, y_after, pltpu.roll(here, 31, 0))
            total = total + jnp.where(first_z, pltpu.roll(here, 65, 1), pltpu.roll(here, 1, 1))
            total = total + jnp.where(last_z, pltpu.roll(here, 63, 1), pltpu.roll(here, 127, 1))
            if f < 4:
                rows = pl.ds(p * 32, 32)
                force_ref[f, rows, :] = chemical_ref[f, rows, :] - total
            else:
                conc_out_ref[p] = conc_ref[p] + STEP_CONC * total[:, :64]
                conc_out_ref[p + 4] = conc_ref[p + 4] + STEP_CONC * total[:, 64:]


VMEM = pl.BlockSpec(memory_space=pltpu.VMEM)
HBM = pl.BlockSpec(memory_space=pltpu.HBM)
ANY = pl.BlockSpec(memory_space=pl.ANY)
LIMIT = 12 * 1024 * 1024


def call(kernel, args, out, scratch=(), special=None, out_spec=VMEM, cost=4e6):
    special = special or {}
    specs = [special.get(i, VMEM) for i in range(len(args))]
    shapes = [jax.ShapeDtypeStruct(s, F32) for s in out]
    return pl.pallas_call(
        kernel,
        out_shape=shapes,
        in_specs=specs,
        out_specs=[out_spec] * len(out),
        scratch_shapes=list(scratch),
        compiler_params=pltpu.CompilerParams(vmem_limit_bytes=LIMIT),
        cost_estimate=pl.CostEstimate(flops=int(cost), bytes_accessed=int(cost), transcendentals=0),
    )(*args)


def exchange(x):
    y = lax.all_to_all(x.reshape(128, 1, 768), BOTH, 0, 0, tiled=True)
    return y.reshape(768, 128)


def step(labels, seed_noise, conc, curvature, quartic, wells, lame, eigen):
    z_tab, z_inv = (jnp.asarray(t) for t in z_tables())
    xf, xi = (jnp.asarray(t) for t in x_tables())
    yt = jnp.asarray(y_tables())

    data = [pltpu.VMEM((768, 256), BF16)]
    plane_scratch = [pltpu.VMEM((384, 384), BF16), pltpu.VMEM((384, 384), BF16)]

    def shift(value, axis, step):
        count = lax.axis_size(axis)
        return lax.ppermute(value, axis, [(i, (i + step) % count) for i in range(count)])

    def spectrum(recv, after):
        (own,) = call(
            spectrum_kernel,
            (recv, xf, yt, *after),
            [(384, 256)],
            plane_scratch,
            {3 + i: ANY for i in range(len(after))},
        )
        return own, lax.ppermute(own, "gx", [(i, i ^ 1) for i in range(16)])

    def update(own, other, after, par):
        (back,) = call(green_kernel, (own, other, after, par, xi, yt), [(768, 128)], plane_scratch, {2: ANY})
        return exchange(back)

    def in_hbm(*arrays):
        return tuple(pltpu.with_memory_space_constraint(a, pltpu.HBM) for a in arrays)

    phase, mat, send, par = call(
        first_kernel,
        in_hbm(labels, seed_noise, lame, eigen, curvature, quartic, wells, z_tab),
        [(4, 128, 128), (8, 128, 128), (768, 128), (48, 128)],
        [
            pltpu.VMEM((8, 32, 64), jnp.int32),
            pltpu.VMEM((4, 8, 32, 64), F32),
            pltpu.SMEM((2, 4), F32),
            pltpu.SMEM((4, 6), F32),
            pltpu.SMEM((4,), F32),
            pltpu.SMEM((4,), F32),
            pltpu.SMEM((4,), F32),
            pltpu.VMEM((2, 128, 384), BF16),
            *data,
            pltpu.SemaphoreType.DMA((8,)),
        ],
        {i: HBM for i in range(8)},
    )
    recv = exchange(send)

    own, other = spectrum(recv, ())
    chem, chemical, xlow, xhigh, ylow, yhigh = call(
        newton_kernel,
        (conc, phase, par, own),
        [(128, 128), (4, 128, 128), (96, 128), (96, 128), (24, 128), (24, 128)],
        special={3: ANY},
    )
    halo = [shift(xhigh, "gx", 1), shift(xlow, "gx", -1), shift(yhigh, "gy", 1), shift(ylow, "gy", -1)]
    back = update(own, other, ylow, par)
    strain, send = call(middle_kernel, (back, mat, z_tab, z_inv), [(6, 128, 128), (768, 128)], data)
    own, other = spectrum(exchange(send), ())
    force, conc_next = call(
        laplace_kernel, (phase, chem, chemical, conc, *halo, own), [(4, 128, 128), (8, 32, 64)], special={8: ANY}
    )
    back = update(own, other, force, par)
    phase_next, stress = call(
        last_kernel,
        (back, phase, mat, strain, force, par, z_inv),
        [(4, 8, 32, 64), (6, 8, 32, 64)],
        [
            pltpu.VMEM((4, 2, 4, 32, 64), F32),
            pltpu.VMEM((4, 2, 6, 32, 64), F32),
            pltpu.SemaphoreType.DMA((16,)),
        ],
        out_spec=HBM,
    )
    return (phase_next, conc_next, stress)


def solution(mesh):
    in_specs = (
        P("gx", "gy", None),
        P(None, "gx", "gy", None),
        P("gx", "gy", None),
        P(),
        P(),
        P(),
        P(),
        P(),
    )
    out_specs = (P(None, "gx", "gy", None), P("gx", "gy", None), P(None, "gx", "gy", None))
    return jax.shard_map(step, mesh=mesh, in_specs=in_specs, out_specs=out_specs, check_vma=False)
```

```python
import numpy as np

import jax
import jax.numpy as jnp
from jax import lax
from jax.experimental import pallas as pl
from jax.experimental.pallas import tpu as pltpu
from jax.sharding import PartitionSpec as P


NEWTON = 5
STEP_PHASE = 0.06
STEP_CONC = 0.005

F32 = jnp.float32
BF16 = jnp.bfloat16

EVEN = (0, 1, 2, 5)
ODD = (3, 4)
ORDER = EVEN + ODD
BOTH = ("gy", "gx")


def split_np(table):
    high = table.astype(np.float32).astype(BF16)
    low = (table - high.astype(np.float64)).astype(np.float32).astype(BF16)
    return high, low


def stack_k(table, axis):
    high, low = split_np(table)
    return np.concatenate([high, high, low], axis=axis)


def z_tables():
    slab = np.arange(64)[:, None]
    z = np.arange(64)[None, :]
    freq = np.where(slab <= 32, slab, slab - 32)
    angle = 2.0 * np.pi * ((freq * z) % 64) / 64.0
    cos, sin = np.cos(angle), np.sin(angle)
    edge = (slab == 0) | (slab == 32)
    first = slab < 32
    even = np.where(edge | first, cos, sin)
    odd = np.where(edge | ~first, cos, sin)
    weight = np.where(edge, 1.0, 2.0) / 64.0

    def double(t):
        return np.kron(np.eye(2), t)

    forward = np.stack([stack_k(double(t), 1) for t in (even, odd)])
    inverse = np.stack([stack_k(double(t * weight), 0) for t in (even, odd)])
    return forward, inverse


def x_tables():
    order = np.array([8 * g + 4 * par + p for par in range(2) for p in range(4) for g in range(8)])
    forward, inverse = [], []
    for parity in range(2):
        k = 2 * np.arange(32)[:, None] + parity
        angle = 2.0 * np.pi * ((k * order[None, :]) % 128) / 128.0
        real, imag = np.cos(angle), -np.sin(angle)
        weight = np.full((64, 1), 2.0)
        if parity == 0:
            imag[0] = np.where(order % 2 == 0, 1.0, -1.0)
            weight[0] = weight[32] = 1.0
        table = np.concatenate([real, imag], axis=0)
        forward.append(stack_k(table, 1))
        inverse.append(stack_k((table * weight / (128.0 * 256.0)).T, 1))
    return np.stack(forward), np.stack(inverse)


def y_tables():
    y = np.arange(128)[:, None]
    m = np.arange(128)[None, :]
    tables = []
    for k, n in ((2 * m, y), (2 * m + 1, y), (2 * y + 1, m)):
        angle = 2.0 * np.pi * ((k * n) % 256) / 256.0
        tables.append(stack_k(np.concatenate([np.cos(angle), np.sin(angle)], axis=1), 0))
    return np.stack(tables)


def split(value):
    high = value.astype(BF16)
    low = (value - high.astype(F32)).astype(BF16)
    return high, low


def dot(a, b, dims=((1,), (0,))):
    return lax.dot_general(a, b, (dims, ((), ())), preferred_element_type=F32)


def dense(low, high):
    return jnp.concatenate([low, high], axis=-1)


class Params:
    def __init__(self, ref):
        self.ref = ref

    def row(self, i):
        return self.ref[pl.ds(i, 1), :]

    def lame(self, i, a):
        return self.row(4 * i + a)

    def eigen(self, a, p):
        return self.row(8 + 6 * a + p)


def write_params(lame, eigen, others, ref):
    def middle(v):
        top = jnp.maximum(jnp.maximum(v[0], v[1]), jnp.maximum(v[2], v[3]))
        least = jnp.minimum(jnp.minimum(v[0], v[1]), jnp.minimum(v[2], v[3]))
        return 0.5 * (top + least)

    values = [lame[i, a] for i in range(2) for a in range(4)]
    values += [eigen[a, p] for a in range(4) for p in range(6)]
    values += [middle(values[0:4]), middle(values[4:8])]
    values += [v[a] for v in others for a in range(4)]
    for i, value in enumerate(values):
        ref[pl.ds(i, 1), :] = jnp.full((1, 128), value, F32)


def material(phase, lame, eigen):
    lam = sum(phase[a] * lame(0, a) for a in range(4))
    shear2 = 2.0 * sum(phase[a] * lame(1, a) for a in range(4))
    eig = [sum(phase[a] * eigen(a, p) for a in range(4)) for p in range(6)]
    return lam, shear2, eig


def stress_from(elastic, lam, shear2):
    trace = lam * (elastic[0] + elastic[1] + elastic[2])
    return [shear2 * elastic[p] + trace if p < 3 else shear2 * elastic[p] for p in range(6)]


def cell_block(b):
    return lax.rem(b + 4 - lax.rem(lax.axis_index("gy"), 4), 4)


def block_rows(p):
    return pl.ds(pl.multiple_of(p * 32, 32), 32)


def put_split(values, b, data_ref):
    for i, c in enumerate(ORDER):
        high, low = split(values[c])
        at = pl.ds(pl.multiple_of(i * 128 + b * 32, 32), 32)
        data_ref[at, :128] = high
        data_ref[at, 128:] = low


NT = ((1,), (1,))


def stack3(value, axis):
    high, low = split(value)
    return jnp.concatenate([high, low, high], axis=axis)


def z_forward(tab_ref, data_ref, send_ref):
    for which, (start, comps) in enumerate(((0, EVEN), (512, ODD))):
        data = data_ref[pl.ds(start, 128 * len(comps)), :]
        out = dot(tab_ref[which], jnp.concatenate([data, data[:, :128]], axis=1), NT)
        for i, c in enumerate(comps):
            r, k = divmod(c, 3)
            for par in range(2):
                piece = out[par * 64 : par * 64 + 64, i * 128 : i * 128 + 128]
                send_ref[pl.ds(r * 6 + k * 2 + par, 64, stride=12), :] = piece


def z_inverse(tab_ref, recv_ref, c):
    r, k = divmod(c, 3)
    pieces = [recv_ref[pl.ds(r * 6 + k * 2 + par, 64, stride=12), :] for par in range(2)]
    data = jnp.concatenate(pieces, axis=0).T
    return dot(stack3(data, 1), tab_ref[int(c in ODD)])


def first_kernel(*refs):
    sources, (phase_ref, mat_ref, send_ref, par_ref), targets, (data_ref, sem) = refs[:8], refs[8:12], refs[12:20], refs[20:]
    copies = [pltpu.make_async_copy(a, b, sem.at[i]) for i, (a, b) in enumerate(zip(sources, targets))]
    for copy in copies:
        copy.start()
    labels_ref, noise_ref, lame_ref, eigen_ref, *others, tab_ref = targets
    for copy in copies[:4]:
        copy.wait()
    by = lax.rem(lax.axis_index("gy"), 4)

    def lame(i, a):
        return lame_ref[i, a]

    def eigen(a, p):
        return eigen_ref[a, p]

    for p in range(4):
        rows = pl.ds(p * 32, 32)
        label = dense(labels_ref[p], labels_ref[p + 4])
        raw = [
            dense(noise_ref[a, p], noise_ref[a, p + 4]) + jnp.where(label == a, 2.0, 0.0).astype(F32)
            for a in range(4)
        ]
        inverse = 1.0 / (raw[0] + raw[1] + raw[2] + raw[3])
        phase = [raw[a] * inverse for a in range(4)]
        for a in range(4):
            phase_ref[a, rows, :] = phase[a]
        lam, shear2, eig = material(phase, lame, eigen)
        for i, value in enumerate([lam, shear2, *eig]):
            mat_ref[i, rows, :] = value
        put_split(stress_from([-v for v in eig], lam, shear2), lax.rem(p + by, 4), data_ref)
    for copy in copies[4:]:
        copy.wait()
    z_forward(tab_ref, data_ref, send_ref)
    write_params(lame_ref, eigen_ref, others, par_ref)


def middle_kernel(recv_ref, mat_ref, tab_ref, inv_ref, strain_ref, send_ref, data_ref):
    strain = []
    for c in range(6):
        strain.append(-z_inverse(inv_ref, recv_ref, c))
        strain_ref[c] = strain[c]
    for b in range(4):
        rows = block_rows(cell_block(b))
        lam, shear2, *eig = [mat_ref[i, rows, :] for i in range(8)]
        elastic = [strain[c][b * 32 : b * 32 + 32] - eig[c] for c in range(6)]
        put_split(stress_from(elastic, lam, shear2), b, data_ref)
    z_forward(tab_ref, data_ref, send_ref)


def last_kernel(
    recv_ref,
    phase_ref,
    mat_ref,
    strain_ref,
    force_ref,
    par_ref,
    inv_ref,
    conc_ref,
    next_hbm,
    stress_hbm,
    conc_hbm,
    next_ref,
    stress_ref,
    sem,
):
    par = Params(par_ref)
    copies = [pltpu.make_async_copy(conc_ref, conc_hbm, sem.at[8])]
    copies[0].start()
    strain = [strain_ref[c] - z_inverse(inv_ref, recv_ref, c) for c in range(6)]
    for b in range(4):
        p = cell_block(b)
        rows = block_rows(p)
        lam, shear2, *eig = [mat_ref[i, rows, :] for i in range(8)]
        elastic = [strain[c][b * 32 : b * 32 + 32] - eig[c] for c in range(6)]
        stress = stress_from(elastic, lam, shear2)
        for c in range(6):
            stress_ref[b, c, 0] = stress[c][:, :64]
            stress_ref[b, c, 1] = stress[c][:, 64:]
        copies.append(pltpu.make_async_copy(stress_ref.at[b], stress_hbm.at[:, :, p], sem.at[2 * b]))
        copies[-1].start()
        trace = elastic[0] + elastic[1] + elastic[2]
        trace = 0.5 * trace * trace
        squares = (
            elastic[0] * elastic[0]
            + elastic[1] * elastic[1]
            + elastic[2] * elastic[2]
            + 2.0 * (elastic[3] * elastic[3] + elastic[4] * elastic[4] + elastic[5] * elastic[5])
        )
        doubled = [stress[c] if c < 3 else 2.0 * stress[c] for c in range(6)]
        force = []
        for a in range(4):
            coupling = sum(doubled[c] * par.eigen(a, c) for c in range(6))
            force.append(force_ref[a, rows, :] + par.lame(0, a) * trace + par.lame(1, a) * squares - coupling)
        mean = 0.25 * (force[0] + force[1] + force[2] + force[3])
        for a in range(4):
            new = phase_ref[a, rows, :] - STEP_PHASE * (force[a] - mean)
            next_ref[b, a, 0] = new[:, :64]
            next_ref[b, a, 1] = new[:, 64:]
        copies.append(pltpu.make_async_copy(next_ref.at[b], next_hbm.at[:, :, p], sem.at[2 * b + 1]))
        copies[-1].start()
    for copy in copies:
        copy.wait()


def mix(x):
    lane = lax.broadcasted_iota(jnp.int32, x[0].shape, 1)
    low = lane < 64
    even = (lane & 32) == 0
    e01, e23, e30, e12 = (jnp.where(even, x[a], x[b]) for a, b in ((0, 1), (2, 3), (3, 0), (1, 2)))
    return [jnp.where(low, a, b) for a, b in ((e01, e23), (e30, e12), (e23, e01), (e12, e30))]


def roll_lanes(x, by):
    return pltpu.roll(x, by, 1) if by else x


def spectrum_kernel(recv_ref, xf_ref, y_ref, *refs):
    *out_refs, even_ref, odd_ref = refs[-4:]
    for k in range(3):
        total, delta = [], []
        for par in range(2):
            columns = []
            for gh in range(2):
                pieces = [recv_ref[pl.ds((4 * gh + i) * 96 + k * 2 + par, 16, stride=6), :] for i in range(4)]
                columns.append([roll_lanes(v, (128 - 32 * p) % 128) for p, v in enumerate(mix(pieces))])
            for p in range(4):
                both = jnp.concatenate([columns[0][p], columns[1][p]], axis=1)
                total.append(both[:8] + both[8:])
                delta.append(both[:8] - both[8:])
        even = dot(xf_ref[0], stack3(jnp.concatenate(total, axis=0), 0))
        odd = dot(xf_ref[1], stack3(jnp.concatenate(delta, axis=0), 0))
        value = jnp.concatenate([even[:32], odd[:32], even[32:], odd[32:]], axis=0)
        left, right = value[:, :128], value[:, 128:]
        rows = pl.ds(k * 128, 128)
        even_ref[rows, :] = stack3(left + right, 1)
        odd_ref[rows, :] = stack3(left - right, 1)
    for which, ref in enumerate((even_ref, odd_ref)):
        mid = dot(ref[...], y_ref[which])
        for k in range(3):
            real, imag = mid[k * 128 : k * 128 + 64], mid[k * 128 + 64 : k * 128 + 128]
            out_refs[which][pl.ds(k * 128, 64), :] = real[:, :128] + imag[:, 128:]
            out_refs[which][pl.ds(k * 128 + 64, 64), :] = imag[:, :128] - real[:, 128:]


def green_tile(re, im, wx, wy, omega, first, second, upper):
    xx, yy, zz, yz, xz, xy = range(6)
    vx = (re[xx] * wx + re[xy] * wy + omega * im[xz], im[xx] * wx + im[xy] * wy - omega * re[xz])
    vy = (re[xy] * wx + re[yy] * wy + omega * im[yz], im[xy] * wx + im[yy] * wy - omega * re[yz])
    vz = (re[xz] * wx + re[yz] * wy - omega * im[zz], im[xz] * wx + im[yz] * wy + omega * re[zz])
    inner = (wx * vx[0] + wy * vy[0] + omega * vz[1], wx * vx[1] + wy * vy[1] - omega * vz[0])
    s = [inner[part] * second for part in range(2)]
    fx = [vx[part] * first for part in range(2)]
    fy = [vy[part] * first for part in range(2)]
    fz = [vz[part] * first for part in range(2)]
    out = []
    for part in range(2):
        other = 1 - part
        if upper:
            sign = -omega if part == 0 else omega
            out.append(
                (
                    wy * fz[part] + sign * (fy[other] - wy * s[other]),
                    wx * fz[part] + sign * (fx[other] - wx * s[other]),
                    wx * (fy[part] - wy * s[part]) + wy * fx[part],
                )
            )
        else:
            turned = fz[1] if part == 0 else -fz[0]
            out.append(
                (
                    wx * (2.0 * fx[part] - wx * s[part]),
                    wy * (2.0 * fy[part] - wy * s[part]),
                    omega * (2.0 * turned - omega * s[part]),
                )
            )
    return out


def green_kernel(*refs):
    own_refs, other_refs = refs[0:2], refs[2:4]
    after_ref, par_ref, xi_ref, y_ref, send_ref, even_ref, odd_ref = refs[4:]
    del after_ref
    x_index, y_index = lax.axis_index("gx"), lax.axis_index("gy")
    core = lax.rem(x_index, 2)
    slab = y_index * 8 + lax.div(x_index, 2)
    omega = jnp.where(slab < 32, slab, 32 - slab).astype(F32) * (1.0 / 64.0)
    par = Params(par_ref)
    lam0 = jnp.concatenate([par.row(32), par.row(32)], axis=1)
    mu0 = jnp.concatenate([par.row(33), par.row(33)], axis=1)
    half_mu = 0.5 / mu0
    ratio = (lam0 + mu0) / (mu0 * (lam0 + 2.0 * mu0))
    lane = lax.broadcasted_iota(jnp.int32, (8, 256), 1)
    index = jnp.where(lane < 128, 2 * lane, 2 * lane - 255)
    index = jnp.where(index == 128, 0, jnp.where(index > 128, index - 256, index))
    wy = index.astype(F32) * (1.0 / 256.0)
    row = lax.broadcasted_iota(jnp.int32, (8, 256), 0)

    def green(upper):
        for tile in range(8):
            wx = (2 * row + (tile % 4 * 16 + tile // 4)).astype(F32) * (1.0 / 128.0)
            q = wx * wx + wy * wy + omega * omega
            inverse = 1.0 / jnp.where(q == 0.0, 1.0, q)
            first = half_mu * inverse
            second = ratio * inverse * inverse

            def get(pair, part):
                rows = [pl.ds(k * 128 + part * 64 + tile * 8, 8) for k in range(3)]
                return [jnp.concatenate([ref[r, :] for ref in pair], axis=1) for r in rows]

            low, high = (other_refs, own_refs) if upper else (own_refs, other_refs)
            re, im = (get(low, part) + get(high, part) for part in range(2))
            out = green_tile(re, im, wx, wy, omega, first, second, upper)
            for part in range(2):
                for k in range(3):
                    at = pl.ds(k * 128 + part * 64 + tile * 8, 8)
                    value = stack3(out[part][k], 0)
                    for i in range(3):
                        piece = value[i * 8 : i * 8 + 8]
                        even_ref[at, i * 128 : i * 128 + 128] = piece[:, :128]
                        odd_ref[at, i * 128 : i * 128 + 128] = piece[:, 128:]

    @pl.when(core == 0)
    def _():
        green(False)

    @pl.when(core == 1)
    def _():
        green(True)

    halves = []
    for ref, table in ((even_ref, y_ref[0]), (odd_ref, y_ref[2])):
        halves.append(dot(ref[...], table))
    for k in range(3):
        sums = []
        for mid in halves:
            real, imag = mid[k * 128 : k * 128 + 64], mid[k * 128 + 64 : k * 128 + 128]
            sums.append((real[:, :128] - imag[:, 128:], imag[:, :128] + real[:, 128:]))
        (re_e, im_e), (re_o, im_o) = sums
        real = jnp.concatenate([re_e + re_o, re_e - re_o], axis=1)
        imag = jnp.concatenate([im_e + im_o, im_e - im_o], axis=1)
        even = dot(xi_ref[0], stack3(jnp.concatenate([real[:32], imag[:32]], axis=0), 0))
        odd = dot(xi_ref[1], stack3(jnp.concatenate([real[32:], imag[32:]], axis=0), 0))
        total, delta = even + odd, even - odd
        for parity in range(2):
            for gh in range(2):
                lanes = slice(gh * 128, gh * 128 + 128)
                pieces = []
                for p in range(4):
                    rows = slice(parity * 32 + p * 8, parity * 32 + p * 8 + 8)
                    pieces.append(
                        roll_lanes(jnp.concatenate([total[rows, lanes], delta[rows, lanes]], axis=0), 32 * p)
                    )
                for i, value in enumerate(mix(pieces)):
                    send_ref[pl.ds((4 * gh + i) * 96 + k * 2 + parity, 16, stride=6), :] = value


def newton_kernel(
    conc_ref,
    phase_ref,
    par_ref,
    after_ref,
    chem_ref,
    chemical_ref,
    xlow_ref,
    xhigh_ref,
    ylow_ref,
    yhigh_ref,
):
    del after_ref
    par = Params(par_ref)
    curvature, quartic, wells = ([par.row(34 + 4 * i + a) for a in range(4)] for i in range(3))
    for p in range(4):
        rows = pl.ds(p * 32, 32)
        conc = dense(conc_ref[p], conc_ref[p + 4])
        phase = [phase_ref[a, rows, :] for a in range(4)]
        part = [conc] * 4
        chem = jnp.zeros_like(conc)
        for a in range(4):
            dev = conc - wells[a]
            chem = chem + phase[a] * (dev * (curvature[a] + quartic[a] * dev * dev))
        for _ in range(NEWTON):
            top = conc
            bottom = jnp.zeros_like(conc)
            slope, recip = [], []
            for a in range(4):
                dev = part[a] - wells[a]
                square = quartic[a] * dev * dev
                g = dev * (curvature[a] + square) - chem
                d = 1.0 / (curvature[a] + 3.0 * square)
                slope.append(g)
                recip.append(d)
                top = top + phase[a] * (g * d - part[a])
                bottom = bottom + phase[a] * d
            shift = top / bottom
            part = [part[a] + (shift - slope[a]) * recip[a] for a in range(4)]
            chem = chem + shift
        chem_ref[rows, :] = chem
        total = sum(phase[a] * phase[a] for a in range(4))
        for a in range(4):
            dev = part[a] - wells[a]
            square = dev * dev
            energy = square * (0.5 * curvature[a] + 0.25 * quartic[a] * square)
            chemical_ref[a, rows, :] = energy - chem * part[a] + 2.0 * phase[a] * (total - phase[a] * phase[a])
    low_half = lax.broadcasted_iota(jnp.int32, (32, 128), 1) < 64

    def field(f, rows):
        return phase_ref[f, rows, :] if f < 4 else chem_ref[rows, :]

    first, last = pl.ds(0, 32), pl.ds(96, 32)
    for j in range(2):
        at = pl.ds(j * 32, 32)
        xlow_ref[at, :] = jnp.where(low_half, field(2 * j, first), pltpu.roll(field(2 * j + 1, first), 64, 1))
        xhigh_ref[at, :] = jnp.where(low_half, pltpu.roll(field(2 * j, last), 64, 1), field(2 * j + 1, last))
    xlow_ref[pl.ds(64, 32), :] = field(4, first)
    xhigh_ref[pl.ds(64, 32), :] = pltpu.roll(field(4, last), 64, 1)
    for f in range(5):
        for p in range(4):
            ylow_ref[pl.ds(f * 4 + p, 1), :] = field(f, pl.ds(p * 32, 1))
            yhigh_ref[pl.ds(f * 4 + p, 1), :] = field(f, pl.ds(p * 32 + 31, 1))
    pad = jnp.zeros((4, 128), F32)
    ylow_ref[pl.ds(20, 4), :] = pad
    yhigh_ref[pl.ds(20, 4), :] = pad


def laplace_kernel(
    phase_ref,
    chem_ref,
    chemical_ref,
    conc_ref,
    xlow_ref,
    xhigh_ref,
    ylow_ref,
    yhigh_ref,
    after_ref,
    force_ref,
    conc_out_ref,
):
    del after_ref
    lane = lax.broadcasted_iota(jnp.int32, (32, 128), 1)
    row = lax.broadcasted_iota(jnp.int32, (32, 128), 0)
    first_z = (lane & 63) == 0
    last_z = (lane & 63) == 63
    low_half = lane < 64
    for f in range(5):
        block = [phase_ref[f, pl.ds(p * 32, 32), :] if f < 4 else chem_ref[pl.ds(p * 32, 32), :] for p in range(4)]
        at = pl.ds(f // 2 * 32, 32)
        before, after = xlow_ref[at, :], xhigh_ref[at, :]
        if f % 2 == 0:
            after = pltpu.roll(after, 64, 1)
        else:
            before = pltpu.roll(before, 64, 1)
        for p in range(4):
            here = block[p]
            total = -6.0 * here
            if p > 0:
                total = total + block[p - 1]
            else:
                total = total + jnp.where(low_half, before, pltpu.roll(block[3], 64, 1))
            if p < 3:
                total = total + block[p + 1]
            else:
                total = total + jnp.where(low_half, pltpu.roll(block[0], 64, 1), after)
            y_before = ylow_ref[pl.ds(f * 4 + p, 1), :]
            y_after = yhigh_ref[pl.ds(f * 4 + p, 1), :]
            total = total + jnp.where(row == 0, y_before, pltpu.roll(here, 1, 0))
            total = total + jnp.where(row == 31, y_after, pltpu.roll(here, 31, 0))
            total = total + jnp.where(first_z, pltpu.roll(here, 65, 1), pltpu.roll(here, 1, 1))
            total = total + jnp.where(last_z, pltpu.roll(here, 63, 1), pltpu.roll(here, 127, 1))
            if f < 4:
                rows = pl.ds(p * 32, 32)
                force_ref[f, rows, :] = chemical_ref[f, rows, :] - total
            else:
                conc_out_ref[p] = conc_ref[p] + STEP_CONC * total[:, :64]
                conc_out_ref[p + 4] = conc_ref[p + 4] + STEP_CONC * total[:, 64:]


VMEM = pl.BlockSpec(memory_space=pltpu.VMEM)
HBM = pl.BlockSpec(memory_space=pltpu.HBM)
ANY = pl.BlockSpec(memory_space=pl.ANY)
LIMIT = 12 * 1024 * 1024


def call(kernel, args, out, scratch=(), special=None, out_spec=VMEM, cost=4e6):
    special = special or {}
    specs = [special.get(i, VMEM) for i in range(len(args))]
    shapes = [jax.ShapeDtypeStruct(s, F32) for s in out]
    return pl.pallas_call(
        kernel,
        out_shape=shapes,
        in_specs=specs,
        out_specs=[out_spec] * len(out),
        scratch_shapes=list(scratch),
        compiler_params=pltpu.CompilerParams(vmem_limit_bytes=LIMIT),
        cost_estimate=pl.CostEstimate(flops=int(cost), bytes_accessed=int(cost), transcendentals=0),
    )(*args)


def exchange(x):
    y = lax.all_to_all(x.reshape(128, 1, 768), BOTH, 0, 0, tiled=True)
    return y.reshape(768, 128)


def step(labels, seed_noise, conc, curvature, quartic, wells, lame, eigen):
    z_tab, z_inv = (jnp.asarray(t) for t in z_tables())
    xf, xi = (jnp.asarray(t) for t in x_tables())
    yt = jnp.asarray(y_tables())

    data = [pltpu.VMEM((768, 256), BF16)]
    plane_scratch = [pltpu.VMEM((384, 384), BF16), pltpu.VMEM((384, 384), BF16)]

    def shift(value, axis, step):
        count = lax.axis_size(axis)
        return lax.ppermute(value, axis, [(i, (i + step) % count) for i in range(count)])

    def spectrum(recv):
        own = call(spectrum_kernel, (recv, xf, yt), [(384, 128)] * 2, plane_scratch)
        return own, [lax.ppermute(v, "gx", [(i, i ^ 1) for i in range(16)]) for v in own]

    def update(own, other, after, par):
        (back,) = call(green_kernel, (*own, *other, after, par, xi, yt), [(768, 128)], plane_scratch, {4: ANY})
        return exchange(back)

    def in_hbm(*arrays):
        return tuple(pltpu.with_memory_space_constraint(a, pltpu.HBM) for a in arrays)

    phase, mat, send, par = call(
        first_kernel,
        in_hbm(labels, seed_noise, lame, eigen, curvature, quartic, wells, z_tab),
        [(4, 128, 128), (8, 128, 128), (768, 128), (48, 128)],
        [
            pltpu.VMEM((8, 32, 64), jnp.int32),
            pltpu.VMEM((4, 8, 32, 64), F32),
            pltpu.SMEM((2, 4), F32),
            pltpu.SMEM((4, 6), F32),
            pltpu.SMEM((4,), F32),
            pltpu.SMEM((4,), F32),
            pltpu.SMEM((4,), F32),
            pltpu.VMEM((2, 128, 384), BF16),
            *data,
            pltpu.SemaphoreType.DMA((8,)),
        ],
        {i: HBM for i in range(8)},
    )
    recv = exchange(send)

    own, other = spectrum(recv)
    chem, chemical, xlow, xhigh, ylow, yhigh = call(
        newton_kernel,
        (conc, phase, par, own[0]),
        [(128, 128), (4, 128, 128), (96, 128), (96, 128), (24, 128), (24, 128)],
        special={3: ANY},
    )
    halo = [shift(xhigh, "gx", 1), shift(xlow, "gx", -1), shift(yhigh, "gy", 1), shift(ylow, "gy", -1)]
    back = update(own, other, ylow, par)
    strain, send = call(middle_kernel, (back, mat, z_tab, z_inv), [(6, 128, 128), (768, 128)], data)
    own, other = spectrum(exchange(send))
    force, conc_next = call(
        laplace_kernel, (phase, chem, chemical, conc, *halo, own[0]), [(4, 128, 128), (8, 32, 64)], special={8: ANY}
    )
    back = update(own, other, force, par)
    phase_next, stress, conc_next = call(
        last_kernel,
        (back, phase, mat, strain, force, par, z_inv, conc_next),
        [(4, 2, 4, 32, 64), (6, 2, 4, 32, 64), (8, 32, 64)],
        [
            pltpu.VMEM((4, 4, 2, 32, 64), F32),
            pltpu.VMEM((4, 6, 2, 32, 64), F32),
            pltpu.SemaphoreType.DMA((9,)),
        ],
        out_spec=HBM,
    )
    return (phase_next.reshape(4, 8, 32, 64), conc_next, stress.reshape(6, 8, 32, 64))


def solution(mesh):
    in_specs = (
        P("gx", "gy", None),
        P(None, "gx", "gy", None),
        P("gx", "gy", None),
        P(),
        P(),
        P(),
        P(),
        P(),
    )
    out_specs = (P(None, "gx", "gy", None), P("gx", "gy", None), P(None, "gx", "gy", None))
    return jax.shard_map(step, mesh=mesh, in_specs=in_specs, out_specs=out_specs, check_vma=False)
```

```python
import numpy as np

import jax
import jax.numpy as jnp
from jax import lax
from jax.experimental import pallas as pl
from jax.experimental.pallas import tpu as pltpu
from jax.sharding import PartitionSpec as P


NEWTON = 5
STEP_PHASE = 0.06
STEP_CONC = 0.005

F32 = jnp.float32
BF16 = jnp.bfloat16

EVEN = (0, 1, 2, 5)
ODD = (3, 4)
ORDER = EVEN + ODD
BOTH = ("gy", "gx")


def split_np(table):
    high = table.astype(np.float32).astype(BF16)
    low = (table - high.astype(np.float64)).astype(np.float32).astype(BF16)
    return high, low


def stack_k(table, axis):
    high, low = split_np(table)
    return np.concatenate([high, high, low], axis=axis)


def z_tables():
    slab = np.arange(64)[:, None]
    z = np.arange(64)[None, :]
    freq = np.where(slab <= 32, slab, slab - 32)
    angle = 2.0 * np.pi * ((freq * z) % 64) / 64.0
    cos, sin = np.cos(angle), np.sin(angle)
    edge = (slab == 0) | (slab == 32)
    first = slab < 32
    even = np.where(edge | first, cos, sin)
    odd = np.where(edge | ~first, cos, sin)
    weight = np.where(edge, 1.0, 2.0) / 64.0

    def double(t):
        return np.kron(np.eye(2), t)

    forward = np.stack([stack_k(double(t), 1) for t in (even, odd)])
    inverse = np.stack([stack_k(double(t * weight), 0) for t in (even, odd)])
    return forward, inverse


def x_tables():
    order = np.array([8 * g + 4 * par + p for par in range(2) for p in range(4) for g in range(8)])
    forward, inverse = [], []
    for parity in range(2):
        k = 2 * np.arange(32)[:, None] + parity
        angle = 2.0 * np.pi * ((k * order[None, :]) % 128) / 128.0
        real, imag = np.cos(angle), -np.sin(angle)
        weight = np.full((64, 1), 2.0)
        if parity == 0:
            imag[0] = np.where(order % 2 == 0, 1.0, -1.0)
            weight[0] = weight[32] = 1.0
        table = np.concatenate([real, imag], axis=0)
        forward.append(stack_k(table, 1))
        inverse.append(stack_k((table * weight / (128.0 * 256.0)).T, 1))
    return np.stack(forward), np.stack(inverse)


def y_tables():
    y = np.arange(128)[:, None]
    m = np.arange(128)[None, :]
    tables = []
    for k, n in ((2 * m, y), (2 * m + 1, y), (2 * y + 1, m)):
        angle = 2.0 * np.pi * ((k * n) % 256) / 256.0
        tables.append(stack_k(np.concatenate([np.cos(angle), np.sin(angle)], axis=1), 0))
    return np.stack(tables)


def split(value):
    high = value.astype(BF16)
    low = (value - high.astype(F32)).astype(BF16)
    return high, low


def dot(a, b, dims=((1,), (0,))):
    return lax.dot_general(a, b, (dims, ((), ())), preferred_element_type=F32)


def dense(low, high):
    return jnp.concatenate([low, high], axis=-1)


class Params:
    def __init__(self, ref):
        self.ref = ref

    def row(self, i):
        return self.ref[pl.ds(i, 1), :]

    def lame(self, i, a):
        return self.row(4 * i + a)

    def eigen(self, a, p):
        return self.row(8 + 6 * a + p)


def write_params(lame, eigen, others, ref):
    def middle(v):
        top = jnp.maximum(jnp.maximum(v[0], v[1]), jnp.maximum(v[2], v[3]))
        least = jnp.minimum(jnp.minimum(v[0], v[1]), jnp.minimum(v[2], v[3]))
        return 0.5 * (top + least)

    values = [lame[i, a] for i in range(2) for a in range(4)]
    values += [eigen[a, p] for a in range(4) for p in range(6)]
    values += [middle(values[0:4]), middle(values[4:8])]
    values += [v[a] for v in others for a in range(4)]
    for i, value in enumerate(values):
        ref[pl.ds(i, 1), :] = jnp.full((1, 128), value, F32)


def material(phase, lame, eigen):
    lam = sum(phase[a] * lame(0, a) for a in range(4))
    shear2 = 2.0 * sum(phase[a] * lame(1, a) for a in range(4))
    eig = [sum(phase[a] * eigen(a, p) for a in range(4)) for p in range(6)]
    return lam, shear2, eig


def stress_from(elastic, lam, shear2):
    trace = lam * (elastic[0] + elastic[1] + elastic[2])
    return [shear2 * elastic[p] + trace if p < 3 else shear2 * elastic[p] for p in range(6)]


def cell_block(b):
    return lax.rem(b + 4 - lax.rem(lax.axis_index("gy"), 4), 4)


def block_rows(p):
    return pl.ds(pl.multiple_of(p * 32, 32), 32)


def put_split(values, b, data_ref):
    for i, c in enumerate(ORDER):
        high, low = split(values[c])
        at = pl.ds(pl.multiple_of(i * 128 + b * 32, 32), 32)
        data_ref[at, :128] = high
        data_ref[at, 128:] = low


NT = ((1,), (1,))


def stack3(value, axis):
    high, low = split(value)
    return jnp.concatenate([high, low, high], axis=axis)


def z_forward(tab_ref, data_ref, send_ref):
    for which, (start, comps) in enumerate(((0, EVEN), (512, ODD))):
        data = data_ref[pl.ds(start, 128 * len(comps)), :]
        out = dot(tab_ref[which], jnp.concatenate([data, data[:, :128]], axis=1), NT)
        for i, c in enumerate(comps):
            r, k = divmod(c, 3)
            for par in range(2):
                piece = out[par * 64 : par * 64 + 64, i * 128 : i * 128 + 128]
                send_ref[pl.ds(r * 6 + k * 2 + par, 64, stride=12), :] = piece


def z_inverse(tab_ref, recv_ref, c):
    r, k = divmod(c, 3)
    pieces = [recv_ref[pl.ds(r * 6 + k * 2 + par, 64, stride=12), :] for par in range(2)]
    data = jnp.concatenate(pieces, axis=0).T
    return dot(stack3(data, 1), tab_ref[int(c in ODD)])


def first_kernel(*refs):
    sources, (phase_ref, mat_ref, send_ref, par_ref), targets, (data_ref, sem) = refs[:8], refs[8:12], refs[12:20], refs[20:]
    copies = [pltpu.make_async_copy(a, b, sem.at[i]) for i, (a, b) in enumerate(zip(sources, targets))]
    for i in (1, 0, 2, 3, 7, 4, 5, 6):
        copies[i].start()
    labels_ref, noise_ref, lame_ref, eigen_ref, *others, tab_ref = targets
    for copy in copies[:4]:
        copy.wait()
    by = lax.rem(lax.axis_index("gy"), 4)

    def lame(i, a):
        return lame_ref[i, a]

    def eigen(a, p):
        return eigen_ref[a, p]

    for p in range(4):
        rows = pl.ds(p * 32, 32)
        label = dense(labels_ref[p], labels_ref[p + 4])
        raw = [
            dense(noise_ref[a, p], noise_ref[a, p + 4]) + jnp.where(label == a, 2.0, 0.0).astype(F32)
            for a in range(4)
        ]
        inverse = 1.0 / (raw[0] + raw[1] + raw[2] + raw[3])
        phase = [raw[a] * inverse for a in range(4)]
        for a in range(4):
            phase_ref[a, rows, :] = phase[a]
        lam, shear2, eig = material(phase, lame, eigen)
        for i, value in enumerate([lam, shear2, *eig]):
            mat_ref[i, rows, :] = value
        put_split(stress_from([-v for v in eig], lam, shear2), lax.rem(p + by, 4), data_ref)
    for copy in copies[4:]:
        copy.wait()
    z_forward(tab_ref, data_ref, send_ref)
    write_params(lame_ref, eigen_ref, others, par_ref)


def middle_kernel(recv_ref, mat_ref, tab_ref, inv_ref, strain_ref, send_ref, data_ref):
    strain = []
    for c in range(6):
        strain.append(-z_inverse(inv_ref, recv_ref, c))
        strain_ref[c] = strain[c]
    for b in range(4):
        rows = block_rows(cell_block(b))
        lam, shear2, *eig = [mat_ref[i, rows, :] for i in range(8)]
        elastic = [strain[c][b * 32 : b * 32 + 32] - eig[c] for c in range(6)]
        put_split(stress_from(elastic, lam, shear2), b, data_ref)
    z_forward(tab_ref, data_ref, send_ref)


def last_kernel(
    recv_ref,
    phase_ref,
    mat_ref,
    strain_ref,
    force_ref,
    par_ref,
    inv_ref,
    conc_ref,
    next_hbm,
    stress_hbm,
    conc_hbm,
    next_ref,
    stress_ref,
    sem,
):
    par = Params(par_ref)
    copies = [pltpu.make_async_copy(conc_ref, conc_hbm, sem.at[8])]
    copies[0].start()
    strain = [strain_ref[c] - z_inverse(inv_ref, recv_ref, c) for c in range(6)]
    for b in range(4):
        p = cell_block(b)
        rows = block_rows(p)
        lam, shear2, *eig = [mat_ref[i, rows, :] for i in range(8)]
        elastic = [strain[c][b * 32 : b * 32 + 32] - eig[c] for c in range(6)]
        stress = stress_from(elastic, lam, shear2)
        for c in range(6):
            stress_ref[b, c, 0] = stress[c][:, :64]
            stress_ref[b, c, 1] = stress[c][:, 64:]
        copies.append(pltpu.make_async_copy(stress_ref.at[b], stress_hbm.at[:, :, p], sem.at[2 * b]))
        copies[-1].start()
        trace = elastic[0] + elastic[1] + elastic[2]
        trace = 0.5 * trace * trace
        squares = (
            elastic[0] * elastic[0]
            + elastic[1] * elastic[1]
            + elastic[2] * elastic[2]
            + 2.0 * (elastic[3] * elastic[3] + elastic[4] * elastic[4] + elastic[5] * elastic[5])
        )
        doubled = [stress[c] if c < 3 else 2.0 * stress[c] for c in range(6)]
        force = []
        for a in range(4):
            coupling = sum(doubled[c] * par.eigen(a, c) for c in range(6))
            force.append(force_ref[a, rows, :] + par.lame(0, a) * trace + par.lame(1, a) * squares - coupling)
        mean = 0.25 * (force[0] + force[1] + force[2] + force[3])
        for a in range(4):
            new = phase_ref[a, rows, :] - STEP_PHASE * (force[a] - mean)
            next_ref[b, a, 0] = new[:, :64]
            next_ref[b, a, 1] = new[:, 64:]
        copies.append(pltpu.make_async_copy(next_ref.at[b], next_hbm.at[:, :, p], sem.at[2 * b + 1]))
        copies[-1].start()
    for copy in copies:
        copy.wait()


def mix(x):
    lane = lax.broadcasted_iota(jnp.int32, x[0].shape, 1)
    low = lane < 64
    even = (lane & 32) == 0
    e01, e23, e30, e12 = (jnp.where(even, x[a], x[b]) for a, b in ((0, 1), (2, 3), (3, 0), (1, 2)))
    return [jnp.where(low, a, b) for a, b in ((e01, e23), (e30, e12), (e23, e01), (e12, e30))]


def roll_lanes(x, by):
    return pltpu.roll(x, by, 1) if by else x


def spectrum_kernel(recv_ref, xf_ref, y_ref, *refs):
    *out_refs, even_ref, odd_ref = refs[-4:]
    for k in range(3):
        total, delta = [], []
        for par in range(2):
            columns = []
            for gh in range(2):
                pieces = [recv_ref[pl.ds((4 * gh + i) * 96 + k * 2 + par, 16, stride=6), :] for i in range(4)]
                columns.append([roll_lanes(v, (128 - 32 * p) % 128) for p, v in enumerate(mix(pieces))])
            for p in range(4):
                both = jnp.concatenate([columns[0][p], columns[1][p]], axis=1)
                total.append(both[:8] + both[8:])
                delta.append(both[:8] - both[8:])
        even = dot(xf_ref[0], stack3(jnp.concatenate(total, axis=0), 0))
        odd = dot(xf_ref[1], stack3(jnp.concatenate(delta, axis=0), 0))
        value = jnp.concatenate([even[:32], odd[:32], even[32:], odd[32:]], axis=0)
        left, right = value[:, :128], value[:, 128:]
        rows = pl.ds(k * 128, 128)
        even_ref[rows, :] = stack3(left + right, 1)
        odd_ref[rows, :] = stack3(left - right, 1)
    for which, ref in enumerate((even_ref, odd_ref)):
        mid = dot(ref[...], y_ref[which])
        for k in range(3):
            real, imag = mid[k * 128 : k * 128 + 64], mid[k * 128 + 64 : k * 128 + 128]
            out_refs[which][pl.ds(k * 128, 64), :] = real[:, :128] + imag[:, 128:]
            out_refs[which][pl.ds(k * 128 + 64, 64), :] = imag[:, :128] - real[:, 128:]


def green_tile(re, im, wx, wy, omega, first, second, upper):
    xx, yy, zz, yz, xz, xy = range(6)
    vx = (re[xx] * wx + re[xy] * wy + omega * im[xz], im[xx] * wx + im[xy] * wy - omega * re[xz])
    vy = (re[xy] * wx + re[yy] * wy + omega * im[yz], im[xy] * wx + im[yy] * wy - omega * re[yz])
    vz = (re[xz] * wx + re[yz] * wy - omega * im[zz], im[xz] * wx + im[yz] * wy + omega * re[zz])
    inner = (wx * vx[0] + wy * vy[0] + omega * vz[1], wx * vx[1] + wy * vy[1] - omega * vz[0])
    s = [inner[part] * second for part in range(2)]
    fx = [vx[part] * first for part in range(2)]
    fy = [vy[part] * first for part in range(2)]
    fz = [vz[part] * first for part in range(2)]
    out = []
    for part in range(2):
        other = 1 - part
        if upper:
            sign = -omega if part == 0 else omega
            out.append(
                (
                    wy * fz[part] + sign * (fy[other] - wy * s[other]),
                    wx * fz[part] + sign * (fx[other] - wx * s[other]),
                    wx * (fy[part] - wy * s[part]) + wy * fx[part],
                )
            )
        else:
            turned = fz[1] if part == 0 else -fz[0]
            out.append(
                (
                    wx * (2.0 * fx[part] - wx * s[part]),
                    wy * (2.0 * fy[part] - wy * s[part]),
                    omega * (2.0 * turned - omega * s[part]),
                )
            )
    return out


def green_kernel(*refs):
    own_refs, other_refs = refs[0:2], refs[2:4]
    after_ref, par_ref, xi_ref, y_ref, send_ref, even_ref, odd_ref = refs[4:]
    del after_ref
    x_index, y_index = lax.axis_index("gx"), lax.axis_index("gy")
    core = lax.rem(x_index, 2)
    slab = y_index * 8 + lax.div(x_index, 2)
    omega = jnp.where(slab < 32, slab, 32 - slab).astype(F32) * (1.0 / 64.0)
    par = Params(par_ref)
    lam0 = jnp.concatenate([par.row(32), par.row(32)], axis=1)
    mu0 = jnp.concatenate([par.row(33), par.row(33)], axis=1)
    half_mu = 0.5 / mu0
    ratio = (lam0 + mu0) / (mu0 * (lam0 + 2.0 * mu0))
    lane = lax.broadcasted_iota(jnp.int32, (8, 256), 1)
    index = jnp.where(lane < 128, 2 * lane, 2 * lane - 255)
    index = jnp.where(index == 128, 0, jnp.where(index > 128, index - 256, index))
    wy = index.astype(F32) * (1.0 / 256.0)
    row = lax.broadcasted_iota(jnp.int32, (8, 256), 0)
    rest = wy * wy + omega * omega

    def green(upper):
        for tile in range(8):
            wx = (2 * row + (tile % 4 * 16 + tile // 4)).astype(F32) * (1.0 / 128.0)
            q = wx * wx + rest
            inverse = 1.0 / jnp.where(q == 0.0, 1.0, q)
            first = half_mu * inverse
            second = ratio * inverse * inverse

            def get(pair, part):
                rows = [pl.ds(k * 128 + part * 64 + tile * 8, 8) for k in range(3)]
                return [jnp.concatenate([ref[r, :] for ref in pair], axis=1) for r in rows]

            low, high = (other_refs, own_refs) if upper else (own_refs, other_refs)
            re, im = (get(low, part) + get(high, part) for part in range(2))
            out = green_tile(re, im, wx, wy, omega, first, second, upper)
            for part in range(2):
                for k in range(3):
                    at = pl.ds(k * 128 + part * 64 + tile * 8, 8)
                    value = stack3(out[part][k], 0)
                    for i in range(3):
                        piece = value[i * 8 : i * 8 + 8]
                        even_ref[at, i * 128 : i * 128 + 128] = piece[:, :128]
                        odd_ref[at, i * 128 : i * 128 + 128] = piece[:, 128:]

    @pl.when(core == 0)
    def _():
        green(False)

    @pl.when(core == 1)
    def _():
        green(True)

    halves = []
    for ref, table in ((even_ref, y_ref[0]), (odd_ref, y_ref[2])):
        halves.append(dot(ref[...], table))
    for k in range(3):
        sums = []
        for mid in halves:
            real, imag = mid[k * 128 : k * 128 + 64], mid[k * 128 + 64 : k * 128 + 128]
            sums.append((real[:, :128] - imag[:, 128:], imag[:, :128] + real[:, 128:]))
        (re_e, im_e), (re_o, im_o) = sums
        real = jnp.concatenate([re_e + re_o, re_e - re_o], axis=1)
        imag = jnp.concatenate([im_e + im_o, im_e - im_o], axis=1)
        even = dot(xi_ref[0], stack3(jnp.concatenate([real[:32], imag[:32]], axis=0), 0))
        odd = dot(xi_ref[1], stack3(jnp.concatenate([real[32:], imag[32:]], axis=0), 0))
        total, delta = even + odd, even - odd
        for parity in range(2):
            for gh in range(2):
                lanes = slice(gh * 128, gh * 128 + 128)
                pieces = []
                for p in range(4):
                    rows = slice(parity * 32 + p * 8, parity * 32 + p * 8 + 8)
                    pieces.append(
                        roll_lanes(jnp.concatenate([total[rows, lanes], delta[rows, lanes]], axis=0), 32 * p)
                    )
                for i, value in enumerate(mix(pieces)):
                    send_ref[pl.ds((4 * gh + i) * 96 + k * 2 + parity, 16, stride=6), :] = value


def newton_kernel(
    conc_ref,
    phase_ref,
    par_ref,
    after_ref,
    chem_ref,
    chemical_ref,
    xlow_ref,
    xhigh_ref,
    ylow_ref,
    yhigh_ref,
):
    del after_ref
    par = Params(par_ref)
    curvature, quartic, wells = ([par.row(34 + 4 * i + a) for a in range(4)] for i in range(3))
    for p in range(4):
        rows = pl.ds(p * 32, 32)
        conc = dense(conc_ref[p], conc_ref[p + 4])
        phase = [phase_ref[a, rows, :] for a in range(4)]
        part = [conc] * 4
        chem = jnp.zeros_like(conc)
        for a in range(4):
            dev = conc - wells[a]
            chem = chem + phase[a] * (dev * (curvature[a] + quartic[a] * dev * dev))
        for _ in range(NEWTON):
            top = conc
            bottom = jnp.zeros_like(conc)
            slope, recip = [], []
            for a in range(4):
                dev = part[a] - wells[a]
                square = quartic[a] * dev * dev
                g = dev * (curvature[a] + square) - chem
                d = 1.0 / (curvature[a] + 3.0 * square)
                slope.append(g)
                recip.append(d)
                top = top + phase[a] * (g * d - part[a])
                bottom = bottom + phase[a] * d
            shift = top / bottom
            part = [part[a] + (shift - slope[a]) * recip[a] for a in range(4)]
            chem = chem + shift
        chem_ref[rows, :] = chem
        total = sum(phase[a] * phase[a] for a in range(4))
        for a in range(4):
            dev = part[a] - wells[a]
            square = dev * dev
            energy = square * (0.5 * curvature[a] + 0.25 * quartic[a] * square)
            chemical_ref[a, rows, :] = energy - chem * part[a] + 2.0 * phase[a] * (total - phase[a] * phase[a])
    low_half = lax.broadcasted_iota(jnp.int32, (32, 128), 1) < 64

    def field(f, rows):
        return phase_ref[f, rows, :] if f < 4 else chem_ref[rows, :]

    first, last = pl.ds(0, 32), pl.ds(96, 32)
    for j in range(2):
        at = pl.ds(j * 32, 32)
        xlow_ref[at, :] = jnp.where(low_half, field(2 * j, first), pltpu.roll(field(2 * j + 1, first), 64, 1))
        xhigh_ref[at, :] = jnp.where(low_half, pltpu.roll(field(2 * j, last), 64, 1), field(2 * j + 1, last))
    xlow_ref[pl.ds(64, 32), :] = field(4, first)
    xhigh_ref[pl.ds(64, 32), :] = pltpu.roll(field(4, last), 64, 1)
    for f in range(5):
        for p in range(4):
            ylow_ref[pl.ds(f * 4 + p, 1), :] = field(f, pl.ds(p * 32, 1))
            yhigh_ref[pl.ds(f * 4 + p, 1), :] = field(f, pl.ds(p * 32 + 31, 1))
    pad = jnp.zeros((4, 128), F32)
    ylow_ref[pl.ds(20, 4), :] = pad
    yhigh_ref[pl.ds(20, 4), :] = pad


def laplace_kernel(
    phase_ref,
    chem_ref,
    chemical_ref,
    conc_ref,
    xlow_ref,
    xhigh_ref,
    ylow_ref,
    yhigh_ref,
    after_ref,
    force_ref,
    conc_out_ref,
):
    del after_ref
    lane = lax.broadcasted_iota(jnp.int32, (32, 128), 1)
    row = lax.broadcasted_iota(jnp.int32, (32, 128), 0)
    first_z = (lane & 63) == 0
    last_z = (lane & 63) == 63
    low_half = lane < 64
    for f in range(5):
        block = [phase_ref[f, pl.ds(p * 32, 32), :] if f < 4 else chem_ref[pl.ds(p * 32, 32), :] for p in range(4)]
        at = pl.ds(f // 2 * 32, 32)
        before, after = xlow_ref[at, :], xhigh_ref[at, :]
        if f % 2 == 0:
            after = pltpu.roll(after, 64, 1)
        else:
            before = pltpu.roll(before, 64, 1)
        for p in range(4):
            here = block[p]
            total = -6.0 * here
            if p > 0:
                total = total + block[p - 1]
            else:
                total = total + jnp.where(low_half, before, pltpu.roll(block[3], 64, 1))
            if p < 3:
                total = total + block[p + 1]
            else:
                total = total + jnp.where(low_half, pltpu.roll(block[0], 64, 1), after)
            y_before = ylow_ref[pl.ds(f * 4 + p, 1), :]
            y_after = yhigh_ref[pl.ds(f * 4 + p, 1), :]
            total = total + jnp.where(row == 0, y_before, pltpu.roll(here, 1, 0))
            total = total + jnp.where(row == 31, y_after, pltpu.roll(here, 31, 0))
            total = total + jnp.where(first_z, pltpu.roll(here, 65, 1), pltpu.roll(here, 1, 1))
            total = total + jnp.where(last_z, pltpu.roll(here, 63, 1), pltpu.roll(here, 127, 1))
            if f < 4:
                rows = pl.ds(p * 32, 32)
                force_ref[f, rows, :] = chemical_ref[f, rows, :] - total
            else:
                conc_out_ref[p] = conc_ref[p] + STEP_CONC * total[:, :64]
                conc_out_ref[p + 4] = conc_ref[p + 4] + STEP_CONC * total[:, 64:]


VMEM = pl.BlockSpec(memory_space=pltpu.VMEM)
HBM = pl.BlockSpec(memory_space=pltpu.HBM)
ANY = pl.BlockSpec(memory_space=pl.ANY)
LIMIT = 12 * 1024 * 1024


def call(kernel, args, out, scratch=(), special=None, out_spec=VMEM, cost=4e6):
    special = special or {}
    specs = [special.get(i, VMEM) for i in range(len(args))]
    shapes = [jax.ShapeDtypeStruct(s, F32) for s in out]
    return pl.pallas_call(
        kernel,
        out_shape=shapes,
        in_specs=specs,
        out_specs=[out_spec] * len(out),
        scratch_shapes=list(scratch),
        compiler_params=pltpu.CompilerParams(vmem_limit_bytes=LIMIT),
        cost_estimate=pl.CostEstimate(flops=int(cost), bytes_accessed=int(cost), transcendentals=0),
    )(*args)


def exchange(x):
    y = lax.all_to_all(x.reshape(128, 1, 768), BOTH, 0, 0, tiled=True)
    return y.reshape(768, 128)


def step(labels, seed_noise, conc, curvature, quartic, wells, lame, eigen):
    z_tab, z_inv = (jnp.asarray(t) for t in z_tables())
    xf, xi = (jnp.asarray(t) for t in x_tables())
    yt = jnp.asarray(y_tables())

    data = [pltpu.VMEM((768, 256), BF16)]
    plane_scratch = [pltpu.VMEM((384, 384), BF16), pltpu.VMEM((384, 384), BF16)]

    def shift(value, axis, step):
        count = lax.axis_size(axis)
        return lax.ppermute(value, axis, [(i, (i + step) % count) for i in range(count)])

    def spectrum(recv):
        own = call(spectrum_kernel, (recv, xf, yt), [(384, 128)] * 2, plane_scratch)
        return own, [lax.ppermute(v, "gx", [(i, i ^ 1) for i in range(16)]) for v in own]

    def update(own, other, after, par):
        (back,) = call(green_kernel, (*own, *other, after, par, xi, yt), [(768, 128)], plane_scratch, {4: ANY})
        return exchange(back)

    def in_hbm(*arrays):
        return tuple(pltpu.with_memory_space_constraint(a, pltpu.HBM) for a in arrays)

    phase, mat, send, par = call(
        first_kernel,
        in_hbm(labels, seed_noise, lame, eigen, curvature, quartic, wells, z_tab),
        [(4, 128, 128), (8, 128, 128), (768, 128), (48, 128)],
        [
            pltpu.VMEM((8, 32, 64), jnp.int32),
            pltpu.VMEM((4, 8, 32, 64), F32),
            pltpu.SMEM((2, 4), F32),
            pltpu.SMEM((4, 6), F32),
            pltpu.SMEM((4,), F32),
            pltpu.SMEM((4,), F32),
            pltpu.SMEM((4,), F32),
            pltpu.VMEM((2, 128, 384), BF16),
            *data,
            pltpu.SemaphoreType.DMA((8,)),
        ],
        {i: HBM for i in range(8)},
    )
    recv = exchange(send)

    own, other = spectrum(recv)
    chem, chemical, xlow, xhigh, ylow, yhigh = call(
        newton_kernel,
        (conc, phase, par, own[0]),
        [(128, 128), (4, 128, 128), (96, 128), (96, 128), (24, 128), (24, 128)],
        special={3: ANY},
    )
    halo = [shift(xhigh, "gx", 1), shift(xlow, "gx", -1), shift(yhigh, "gy", 1), shift(ylow, "gy", -1)]
    back = update(own, other, ylow, par)
    strain, send = call(middle_kernel, (back, mat, z_tab, z_inv), [(6, 128, 128), (768, 128)], data)
    own, other = spectrum(exchange(send))
    force, conc_next = call(
        laplace_kernel, (phase, chem, chemical, conc, *halo, own[0]), [(4, 128, 128), (8, 32, 64)], special={8: ANY}
    )
    back = update(own, other, force, par)
    phase_next, stress, conc_next = call(
        last_kernel,
        (back, phase, mat, strain, force, par, z_inv, conc_next),
        [(4, 2, 4, 32, 64), (6, 2, 4, 32, 64), (8, 32, 64)],
        [
            pltpu.VMEM((4, 4, 2, 32, 64), F32),
            pltpu.VMEM((4, 6, 2, 32, 64), F32),
            pltpu.SemaphoreType.DMA((9,)),
        ],
        out_spec=HBM,
    )
    return (phase_next.reshape(4, 8, 32, 64), conc_next, stress.reshape(6, 8, 32, 64))


def solution(mesh):
    in_specs = (
        P("gx", "gy", None),
        P(None, "gx", "gy", None),
        P("gx", "gy", None),
        P(),
        P(),
        P(),
        P(),
        P(),
    )
    out_specs = (P(None, "gx", "gy", None), P("gx", "gy", None), P(None, "gx", "gy", None))
    return jax.shard_map(step, mesh=mesh, in_specs=in_specs, out_specs=out_specs, check_vma=False)
```
